32 devices in a mesh: dp: 4 (over y, x), seq: 4 (over z), tp: 2 (over core).
Axes of the slice: x: 2, y: 2, z: 4, core: 2. Of those that a mesh axis runs over, the one named last changes fastest.
Arguments:
- queries: bfloat16 [4, 2048, 5120], P('dp', 'seq', 'tp'), may hold values from -200 to 200
- keys: bfloat16 [4, 512, 5120], P('dp', None, 'tp'), may hold values from -6 to 6
- values: bfloat16 [4, 512, 5120], P('dp', None, 'tp'), may hold values from -6 to 6
- grad_attention: bfloat16 [4, 2048, 5120], P('dp', 'seq', 'tp'), may hold values from -48 to 48
- normed: bfloat16 [4, 512, 4096], P('dp', None, 'seq'), may hold values from -6 to 6
- norm_scale: float32 [4, 512], P('dp'), may hold values from 0.3 to 3
- norm_gain: float32 [4096], P('seq'), may hold values from 0.1 to 1.9
- key_weight: bfloat16 [4096, 5120], P('seq', 'tp'), may hold values from -0.078125 to 0.078125
- value_weight: bfloat16 [4096, 5120], P('seq', 'tp'), may hold values from -0.078125 to 0.078125
- key_down: bfloat16 [4096, 32], P('seq'), may hold values from -0.09375 to 0.09375
- key_up: bfloat16 [32, 5120], P(None, 'tp'), may hold values from -0.078125 to 0.078125
- value_down: bfloat16 [4096, 32], P('seq'), may hold values from -0.09375 to 0.09375
- value_up: bfloat16 [32, 5120], P(None, 'tp'), may hold values from -0.078125 to 0.078125
- out_weight: bfloat16 [10240, 4096], P('tp', 'seq'), may hold values from -0.09375 to 0.09375
Outputs:
- grad_queries: bfloat16 [4, 2048, 5120], P('dp', 'seq', 'tp')
- grad_text: bfloat16 [4, 512, 4096], P('dp', None, 'seq')
- grad_hidden: bfloat16 [4, 512, 10240], P('dp', 'seq', 'tp')
- grad_key_down: float32 [4096, 32], P('seq')
- grad_key_up: float32 [32, 5120], P(None, 'tp')
- grad_value_down: float32 [4096, 32], P('seq')
- grad_value_up: float32 [32, 5120], P(None, 'tp')
The draws below stay inside these ranges and needn't reach their ends.
All inputs are finite; a program needn't handle non-finite values.
Results may differ from the reference program's by a relative error of at most 0.03.
Values may be sent and summed in bfloat16 or wider, within the bound.
A program may use at most 192 MiB of HBM per device.

```python
import math
import jax
import jax.numpy as jnp
from jax import lax

D = 5120
H = 40
HD = 128
DT = 4096
FF = 10240
R = 32
LTXT = 512
IMG_DEV = 512
IMG = 2048
PROMPTS = 4
N_SEQ = 4


def key_table(key):
    table = jnp.clip(jax.random.normal(jax.random.fold_in(key, 101), (PROMPTS, LTXT, D), jnp.float32), -5.0, 5.0)
    return table


def draw_keys(key, part):
    return key_table(key).astype(jnp.bfloat16)


def draw_queries(key, part):
    table = jnp.clip(jax.random.normal(jax.random.fold_in(key, 103), (PROMPTS, IMG, D), jnp.float32), -5.0, 5.0)
    return table.astype(jnp.bfloat16)


def levels(own_key, dims, shards, low, high):
    gain, own = 1.0, jax.random.fold_in(own_key, 6)
    for position, parts in shards:
        steps = jnp.exp(jax.random.uniform(jax.random.fold_in(own, position), (parts,), jnp.float32, low / len(shards), high / len(shards)))
        gain = gain * jnp.repeat(steps, dims[position] // parts).reshape([-1 if axis == position else 1 for axis in range(len(dims))])
    return gain


def gaussian(key, dims, deviation, most, pieces=(), kind=jnp.bfloat16):
    level = levels(key, dims, pieces, -0.22, 0.18) if pieces else 1.0
    drawn = jax.random.normal(key, dims, jnp.float32) * deviation * level
    return jnp.minimum(jnp.maximum(drawn, -most), most).astype(kind)


def setup_inputs(seed: int = 0) -> dict:
    streams_of = jax.random.split(jax.random.key(seed), 15)
    queries = draw_queries(jax.random.fold_in(streams_of[14], 71), 0)
    keys = draw_keys(jax.random.fold_in(streams_of[14], 71), 0)
    values = gaussian(streams_of[2], (PROMPTS, LTXT, D), 1.0, 6.0, ((0, 4), (2, 2)))
    grad_attention = gaussian(streams_of[3], (PROMPTS, IMG, D), 8.0, 48.0, ((0, 4), (1, 4), (2, 2)))
    normed = gaussian(streams_of[4], (PROMPTS, LTXT, DT), 1.0, 6.0, ((0, 4), (2, 4)))
    norm_scale = jnp.clip(jnp.exp(math.log(3.0) - 2.3025851 * jax.random.uniform(streams_of[5], (PROMPTS, LTXT), jnp.float32) ** levels(streams_of[5], (PROMPTS, LTXT), ((0, 4),), -0.2, 0.2)), 0.3, 3.0)
    norm_gain = jnp.clip(1.0 + 0.18 * jax.random.normal(streams_of[6], (DT,), jnp.float32), 0.1, 1.9)
    key_weight = gaussian(streams_of[7], (DT, D), D ** -0.5, 0.078125, ((0, 4), (1, 2)))
    value_weight = gaussian(streams_of[8], (DT, D), D ** -0.5, 0.078125, ((0, 4), (1, 2)))
    key_down = gaussian(streams_of[9], (DT, R), DT ** -0.5, 0.09375, ((0, 4),))
    key_up = gaussian(streams_of[10], (R, D), D ** -0.5, 0.078125, ((1, 2),))
    value_down = gaussian(streams_of[11], (DT, R), DT ** -0.5, 0.09375, ((0, 4),))
    value_up = gaussian(streams_of[12], (R, D), D ** -0.5, 0.078125, ((1, 2),))
    out_weight = gaussian(streams_of[13], (FF, DT), DT ** -0.5, 0.09375, ((0, 2), (1, 4)))
    return dict(queries=queries, keys=keys, values=values, grad_attention=grad_attention, normed=normed, norm_scale=norm_scale, norm_gain=norm_gain, key_weight=key_weight, value_weight=value_weight, key_down=key_down, key_up=key_up, value_down=value_down, value_up=value_up, out_weight=out_weight)


def settle(partial_values):
    return lax.optimization_barrier(partial_values.astype(jnp.bfloat16)).astype(jnp.float32)


def head_grads(operands):
    query_rows, key_rows, value_rows, grad_rows = operands
    factor = HD ** -0.5
    scores = jnp.dot(query_rows, key_rows.T, preferred_element_type=jnp.float32) * factor
    weights = jnp.exp(scores - jnp.max(scores, axis=1, keepdims=True))
    probability = weights / jnp.sum(weights, axis=1, keepdims=True)
    weights_low = probability.astype(jnp.bfloat16)
    grad_probs = jnp.dot(grad_rows, value_rows.T, preferred_element_type=jnp.float32)
    grad_scores = probability * (grad_probs - jnp.sum(probability * grad_probs, axis=1, keepdims=True))
    grad_low = grad_scores.astype(jnp.bfloat16)
    grad_query = (jnp.dot(grad_low, key_rows, preferred_element_type=jnp.float32) * factor).astype(jnp.bfloat16)
    low_blocks = grad_low.reshape(N_SEQ, IMG_DEV, LTXT).astype(jnp.float32)
    weight_blocks = weights_low.reshape(N_SEQ, IMG_DEV, LTXT).astype(jnp.float32)
    query_blocks = query_rows.reshape(N_SEQ, IMG_DEV, HD).astype(jnp.float32)
    grad_blocks = grad_rows.reshape(N_SEQ, IMG_DEV, HD).astype(jnp.float32)
    grad_key = jnp.sum(settle(jnp.einsum("sij,sid->sjd", low_blocks, query_blocks) * factor), axis=0)
    grad_value = jnp.sum(settle(jnp.einsum("sij,sid->sjd", weight_blocks, grad_blocks)), axis=0)
    return grad_query, grad_key, grad_value


def block_latent(context, down_factor):
    slab_width = DT // N_SEQ
    context_blocks = context.reshape(LTXT, N_SEQ, slab_width).transpose(1, 0, 2).astype(jnp.float32)
    down_blocks = down_factor.reshape(N_SEQ, slab_width, R).astype(jnp.float32)
    return jnp.sum(settle(jnp.einsum("slc,scr->slr", context_blocks, down_blocks)), axis=0).astype(jnp.bfloat16)


def reference(queries, keys, values, grad_attention, normed, norm_scale, norm_gain, key_weight, value_weight, key_down, key_up, value_down, value_up, out_weight):
    slab_width = DT // N_SEQ
    query_list, text_list, hidden_list = [], [], []
    key_down_sum = jnp.zeros((DT, R), jnp.float32)
    value_down_sum = jnp.zeros((DT, R), jnp.float32)
    key_up_sum = jnp.zeros((R, D), jnp.float32)
    value_up_sum = jnp.zeros((R, D), jnp.float32)
    for prompt in range(PROMPTS):
        query_heads = queries[prompt].reshape(IMG, H, HD).transpose(1, 0, 2)
        key_heads = keys[prompt].reshape(LTXT, H, HD).transpose(1, 0, 2)
        value_heads = values[prompt].reshape(LTXT, H, HD).transpose(1, 0, 2)
        grad_heads = grad_attention[prompt].reshape(IMG, H, HD).transpose(1, 0, 2)
        grad_query, grad_key, grad_value = lax.map(head_grads, (query_heads, key_heads, value_heads, grad_heads))
        query_list.append(grad_query.transpose(1, 0, 2).reshape(IMG, D))
        key_grad = grad_key.transpose(1, 0, 2).reshape(LTXT, D).astype(jnp.bfloat16)
        value_grad = grad_value.transpose(1, 0, 2).reshape(LTXT, D).astype(jnp.bfloat16)
        context = (normed[prompt].astype(jnp.float32) * norm_gain).astype(jnp.bfloat16)
        key_latent = block_latent(context, key_down)
        value_latent = block_latent(context, value_down)
        key_back = jnp.dot(key_grad, key_up.T, preferred_element_type=jnp.float32).astype(jnp.bfloat16)
        value_back = jnp.dot(value_grad, value_up.T, preferred_element_type=jnp.float32).astype(jnp.bfloat16)
        grad_context = jnp.dot(key_grad, key_weight.T, preferred_element_type=jnp.float32)
        grad_context = grad_context + jnp.dot(value_grad, value_weight.T, preferred_element_type=jnp.float32)
        grad_context = grad_context + jnp.dot(key_back, key_down.T, preferred_element_type=jnp.float32)
        grad_context = grad_context + jnp.dot(value_back, value_down.T, preferred_element_type=jnp.float32)
        text_rows = normed[prompt].astype(jnp.float32)
        scaled = norm_gain * grad_context
        token_sum = jnp.sum(text_rows * scaled, axis=1, keepdims=True)
        grad_text = (norm_scale[prompt][:, None] * (scaled - text_rows * token_sum / DT)).astype(jnp.bfloat16)
        text_list.append(grad_text)
        hidden = jnp.zeros((LTXT, FF), jnp.float32)
        for block_index in range(N_SEQ):
            offset = block_index * slab_width
            hidden = hidden + settle(jnp.dot(grad_text[:, offset:offset + slab_width], out_weight[:, offset:offset + slab_width].T, preferred_element_type=jnp.float32))
        hidden_list.append(hidden.astype(jnp.bfloat16))
        key_down_sum = key_down_sum + jnp.dot(context.T, key_back, preferred_element_type=jnp.float32)
        value_down_sum = value_down_sum + jnp.dot(context.T, value_back, preferred_element_type=jnp.float32)
        key_up_sum = key_up_sum + jnp.dot(key_latent.T, key_grad, preferred_element_type=jnp.float32)
        value_up_sum = value_up_sum + jnp.dot(value_latent.T, value_grad, preferred_element_type=jnp.float32)
    return (jnp.stack(query_list), jnp.stack(text_list), jnp.stack(hidden_list), key_down_sum / PROMPTS, key_up_sum / PROMPTS, value_down_sum / PROMPTS, value_up_sum / PROMPTS)
```

```python
import functools

import jax
import jax.numpy as jnp
from jax import lax
from jax.experimental import pallas as pl
from jax.experimental.pallas import tpu as pltpu
from jax.sharding import PartitionSpec as P

HD = 128
MESH = pl.DeviceIdType.MESH
LOW = jnp.bfloat16


def dot(left_side, right_side, left_dim, right_dim):
    return lax.dot_general(
        left_side,
        right_side,
        (((left_dim,), (right_dim,)), ((), ())),
        preferred_element_type=jnp.float32,
    )


def exchange(axis, size, landing, send, recv):
    me = lax.axis_index(axis)

    def copy(slot, offset):
        return pltpu.make_async_remote_copy(
            src_ref=landing.at[slot],
            dst_ref=landing.at[slot],
            send_sem=send.at[offset],
            recv_sem=recv.at[slot],
            device_id={axis: lax.rem(me + offset, size)},
            device_id_type=MESH,
        )

    def start():
        for offset in range(1, size):
            copy(me, offset).start()

    def finish():
        for offset in range(1, size):
            copy(lax.rem(me + offset, size), offset).wait_recv()
        for offset in range(1, size):
            copy(me, offset).wait_send()

    return start, finish


def low_sum(ref, size):
    value = ref[0].astype(jnp.float32)
    for index in range(1, size):
        value = value + ref[index].astype(jnp.float32)
    return value


def kernel(
    plan,
    queries,
    keys,
    values,
    grads,
    key_weight,
    value_weight,
    key_up,
    value_up,
    out_weight,
    normed,
    scale,
    gain,
    key_down,
    value_down,
    grad_query,
    grad_hidden,
    grad_text,
    key_down_grad,
    value_down_grad,
    key_up_grad,
    value_up_grad,
    part,
    up_in,
    up_out,
    down_in,
    down_out,
    total,
    project,
    context_all,
    project_all,
    text,
    sum_all,
    latent_own,
    latent_all,
    latent,
    up_sum,
    up_all,
    rows_all,
    down_sum,
    down_all,
    up_send,
    up_recv,
    down_send,
    down_recv,
    high_send,
    high_recv,
    low_send,
    low_recv,
    context_send,
    context_recv,
    project_send,
    project_recv,
    sum_send,
    sum_recv,
    latent_send,
    latent_recv,
    up_dp_send,
    up_dp_recv,
    down_dp_send,
    down_dp_recv,
    rows_send,
    rows_recv,
    text_sem,
):
    n, splits, prompts = plan["n"], plan["splits"], plan["prompts"]
    heads, slices, lag = plan["heads"], plan["slices"], plan["lag"]
    first, second, steps = plan["first"], plan["second"], plan["steps"]
    length, features = normed.shape
    block = length // n
    sub = block // 2
    half_length = length // 2
    rank = key_down.shape[0]
    step = pl.program_id(0)
    me = lax.axis_index("seq")
    split = lax.axis_index("tp")
    prompt = lax.axis_index("dp")
    factor = HD ** (-0.5)
    above = lax.rem(me + 1, n)
    below = lax.rem(me + n - 1, n)
    has_low = me > 0
    has_high = me < n - 1

    def rows_of(value, half):
        return jnp.concatenate(
            [
                value[owner * block + half * sub : owner * block + half * sub + sub]
                for owner in range(n)
            ],
            axis=0,
        )

    def context_of(half):
        return (rows_of(normed, half).astype(jnp.float32) * gain[...]).astype(LOW)

    def column(row, size):
        return jnp.transpose(jnp.broadcast_to(row, (128, size)))[:, :1]

    def up_copy(half, index, source):
        return pltpu.make_async_remote_copy(
            src_ref=source.at[half, index],
            dst_ref=up_in.at[half, index],
            send_sem=up_send.at[half, index],
            recv_sem=up_recv.at[half, index],
            device_id={"seq": above},
            device_id_type=MESH,
        )

    def down_copy(half, index, source):
        return pltpu.make_async_remote_copy(
            src_ref=source.at[half, index],
            dst_ref=down_in.at[half, index],
            send_sem=down_send.at[half, index],
            recv_sem=down_recv.at[half, index],
            device_id={"seq": below},
            device_id_type=MESH,
        )

    def high_copy(half, index, source, owner):
        rows = pl.ds(owner * sub, (n - owner) * sub)
        return pltpu.make_async_remote_copy(
            src_ref=source.at[half, index, :, rows],
            dst_ref=up_in.at[half, index, :, rows],
            send_sem=high_send.at[half, index],
            recv_sem=high_recv.at[half, index],
            device_id={"seq": above},
            device_id_type=MESH,
        )

    def low_copy(half, index, source, owner):
        rows = pl.ds(0, (owner + 1) * sub)
        return pltpu.make_async_remote_copy(
            src_ref=source.at[half, index, :, rows],
            dst_ref=down_in.at[half, index, :, rows],
            send_sem=low_send.at[half, index],
            recv_sem=low_recv.at[half, index],
            device_id={"seq": below},
            device_id_type=MESH,
        )

    def attend(position):
        live = jnp.logical_and(position >= 0, position < 2 * heads)
        half = (position >= heads).astype(jnp.int32)
        return live, half, position - half * heads

    def hide(position):
        live = jnp.logical_or(
            jnp.logical_and(position >= first, position < first + slices),
            jnp.logical_and(position >= second, position < second + slices),
        )
        half = (position >= second).astype(jnp.int32)
        return live, half, position - first - half * (second - first)

    @pl.when(step == 0)
    def _():
        barrier = pltpu.get_barrier_semaphore()
        for axis, size in (("tp", splits), ("seq", n), ("dp", prompts)):
            for offset in range(1, size):
                pl.semaphore_signal(
                    barrier,
                    inc=1,
                    device_id={axis: lax.rem(lax.axis_index(axis) + offset, size)},
                    device_id_type=MESH,
                )
        pl.semaphore_wait(barrier, splits + n + prompts - 3)

    @pl.when(step < heads)
    def _():
        query, key, value, grad = queries[...], keys[...], values[...], grads[...]
        scores = dot(key, query, 1, 1) * factor
        weights = jnp.exp(scores - jnp.max(scores, axis=0, keepdims=True))
        probability = weights * (1.0 / jnp.sum(weights, axis=0, keepdims=True))
        value_part = dot(probability.astype(LOW), grad, 1, 0).astype(LOW)
        grad_probs = dot(value, grad, 1, 1)
        grad_scores = probability * (
            grad_probs - jnp.sum(probability * grad_probs, axis=0, keepdims=True)
        )
        grad_low = grad_scores.astype(LOW)
        key_part = (dot(grad_low, query, 1, 0) * factor).astype(LOW)
        for kind, side in ((0, key_part), (1, value_part)):
            for half in range(2):
                part[half, step, kind] = rows_of(side, half)
        grad_query[...] = (dot(grad_low, key, 0, 0) * factor).astype(LOW)

    live, half, index = hide(step)

    @pl.when(live)
    def _():
        product = dot(text[half].reshape(half_length, features), out_weight[...], 1, 1)
        product = product.astype(LOW)
        part[half, index, 0] = product[:, :HD]
        part[half, index, 1] = product[:, HD:]

    up_at = step - 2 * me
    down_at = step - 2 * (n - 1 - me)

    live, half, index = attend(up_at)

    @pl.when(jnp.logical_and(live, me == 0))
    def _():
        up_copy(half, index, part).start()
        up_in[half, index] = jnp.zeros(up_in.shape[2:], LOW)

    @pl.when(jnp.logical_and(live, has_low))
    def _():
        up_copy(half, index, up_out).wait_recv()

        @pl.when(has_high)
        def _():
            up_out[half, index] = up_in[half, index] + part[half, index]
            up_copy(half, index, up_out).start()

    live, half, index = attend(down_at)

    @pl.when(jnp.logical_and(live, me == n - 1))
    def _():
        down_copy(half, index, part).start()
        down_in[half, index] = jnp.zeros(down_in.shape[2:], LOW)

    @pl.when(jnp.logical_and(live, has_high))
    def _():
        down_copy(half, index, down_out).wait_recv()

        @pl.when(has_low)
        def _():
            down_out[half, index] = down_in[half, index] + part[half, index]
            down_copy(half, index, down_out).start()

    live, half, index = hide(up_at)
    for place in range(n):

        @pl.when(jnp.logical_and(live, me == place))
        def _():
            if place > 0:
                high_copy(half, index, up_out, place).wait_recv()
            else:
                up_in[half, index, :, :sub] = jnp.zeros((2, sub, HD), LOW)
            if place < n - 1:
                rest = (place + 1) * sub
                if place > 0:
                    up_out[half, index, :, rest:] = (
                        up_in[half, index, :, rest:] + part[half, index, :, rest:]
                    )
                high_copy(half, index, up_out if place > 0 else part, place + 1).start()

    live, half, index = hide(down_at)
    for place in range(n):

        @pl.when(jnp.logical_and(live, me == place))
        def _():
            if place < n - 1:
                low_copy(half, index, down_out, place).wait_recv()
            else:
                down_in[half, index, :, place * sub :] = jnp.zeros((2, sub, HD), LOW)
            if place > 0:
                rest = place * sub
                if place < n - 1:
                    down_out[half, index, :, :rest] = (
                        down_in[half, index, :, :rest] + part[half, index, :, :rest]
                    )
                low_copy(half, index, down_out if place < n - 1 else part, place - 1).start()

    @pl.when(step == 0)
    def _():
        total[...] = jnp.zeros_like(total)
        project[...] = jnp.zeros_like(project)
        up_sum[...] = jnp.zeros_like(up_sum)

    def latent_copy(slot, owner, offset):
        return pltpu.make_async_remote_copy(
            src_ref=latent_own.at[owner],
            dst_ref=latent_all.at[slot],
            send_sem=latent_send.at[offset],
            recv_sem=latent_recv.at[slot],
            device_id={"seq": lax.rem(me + offset, n)},
            device_id_type=MESH,
        )

    @pl.when(step == 1)
    def _():
        down = jnp.concatenate([key_down[...], value_down[...]], axis=0)
        sides = [dot(down, context_of(side), 1, 1) for side in range(2)]
        latent_own[...] = (
            jnp.concatenate(sides, axis=1).reshape(latent_own.shape).astype(LOW)
        )
        for offset in range(1, n):
            latent_copy(me, lax.rem(me + offset, n), offset).start()
        latent_all[me] = latent_own[me]

    @pl.when(step == lag - 1)
    def _():
        for offset in range(1, n):
            latent_copy(lax.rem(me + offset, n), me, offset).wait_recv()
        for offset in range(1, n):
            latent_copy(me, lax.rem(me + offset, n), offset).wait_send()
        both = low_sum(latent_all, n).astype(LOW)
        for side in range(2):
            latent[side] = both[:, side * half_length : (side + 1) * half_length]

    live, half, index = attend(step - lag)

    @pl.when(live)
    def _():
        @pl.when(has_high)
        def _():
            up_copy(half, index, up_out).wait_send()

        @pl.when(has_low)
        def _():
            down_copy(half, index, down_out).wait_send()

        both = (
            up_in[half, index].astype(jnp.float32)
            + part[half, index].astype(jnp.float32)
            + down_in[half, index].astype(jnp.float32)
        ).astype(LOW)
        pair = jnp.concatenate([both[0], both[1]], axis=1)
        slab = jnp.concatenate([key_weight[...], value_weight[...]], axis=1)
        total[half] += dot(pair, slab, 1, 1)
        blank = jnp.zeros((rank, HD), LOW)
        rises = jnp.concatenate(
            [
                jnp.concatenate([key_up[...], blank], axis=1),
                jnp.concatenate([blank, value_up[...]], axis=1),
            ],
            axis=0,
        )
        project[half] += dot(pair, rises, 1, 1)
        own = jnp.where(me < n // 2, both[0], both[1])
        up_sum[index] += dot(latent[half], own, 1, 0)

    for side in range(2):
        end = heads * (side + 1) + lag - 1
        project_start, project_finish = exchange(
            "tp", splits, project_all.at[side], project_send.at[side], project_recv.at[side]
        )
        context_start, context_finish = exchange(
            "tp", splits, context_all.at[side], context_send.at[side], context_recv.at[side]
        )
        sum_start, sum_finish = exchange(
            "seq", n, sum_all.at[side], sum_send.at[side], sum_recv.at[side]
        )

        @pl.when(step == end)
        def _():
            project_all[side, split] = project[side].astype(LOW)
            context_all[side, split] = total[side].astype(LOW)
            project_start()
            context_start()

        @pl.when(step == end + 2)
        def _():
            project_finish()
            context_finish()
            back = low_sum(project_all.at[side], splits).astype(LOW)
            low_rank = dot(back[:, :rank], key_down[...], 1, 0) + dot(
                back[:, rank:], value_down[...], 1, 0
            )
            scaled = gain[...] * (low_sum(context_all.at[side], splits) + low_rank)
            total[side] = scaled
            local_sum = jnp.sum(
                rows_of(normed, side).astype(jnp.float32) * scaled, axis=1, keepdims=True
            )
            sum_all[side, me] = jnp.transpose(jnp.broadcast_to(local_sum, (half_length, 128)))[
                :8, :
            ]
            sum_start()
            down = dot(back, context_of(side), 0, 0)
            if side == 0:
                down_sum[...] = down
            else:
                down_sum[...] += down

        @pl.when(step == end + 6)
        def _():
            sum_finish()
            token_sum = sum_all[side, 0]
            for other in range(1, n):
                token_sum = token_sum + sum_all[side, other]
            token_column = column(token_sum[:1, :], half_length)
            result = rows_of(column(scale[...], length), side) * (
                total[side]
                - rows_of(normed, side).astype(jnp.float32)
                * (token_column / plan["features_whole"])
            )
            text[side] = result.astype(LOW).reshape(n, sub, features)
            for owner in range(n):
                pltpu.make_async_copy(
                    text.at[side, owner],
                    grad_text.at[pl.ds(owner * block + side * sub, sub)],
                    text_sem.at[side, owner],
                ).start()

    end = 2 * heads + lag - 1
    up_start, up_finish = exchange("dp", prompts, up_all, up_dp_send, up_dp_recv)
    down_start, down_finish = exchange("dp", prompts, down_all, down_dp_send, down_dp_recv)
    rows_start, rows_finish = exchange("seq", n, rows_all, rows_send, rows_recv)

    @pl.when(step == end + 1)
    def _():
        up_all[prompt] = jnp.concatenate(
            [up_sum[index] for index in range(heads)], axis=1
        ).astype(LOW)
        up_start()

    @pl.when(step == end + 3)
    def _():
        down_all[prompt] = down_sum[...].astype(LOW)
        down_start()

    @pl.when(step == end + 7)
    def _():
        up_finish()
        rows_all[me] = (low_sum(up_all, prompts) / prompts).astype(LOW)
        rows_start()

    @pl.when(step == end + 9)
    def _():
        down_finish()
        down = low_sum(down_all, prompts)
        key_down_grad[...] = down[:rank] / prompts
        value_down_grad[...] = down[rank:] / prompts

    @pl.when(step == end + 14)
    def _():
        rows_finish()
        key_up_grad[...] = rows_all[: n // 2].astype(jnp.float32).reshape(key_up_grad.shape)
        value_up_grad[...] = rows_all[n // 2 :].astype(jnp.float32).reshape(value_up_grad.shape)

    live, half, index = hide(step - lag)
    for place in range(n):

        @pl.when(jnp.logical_and(live, me == place))
        def _():
            if place < n - 1:
                high_copy(half, index, up_out, place + 1).wait_send()
            if place > 0:
                low_copy(half, index, down_out, place - 1).wait_send()
            own = slice(place * sub, (place + 1) * sub)
            both = (
                up_in[half, index, :, own].astype(jnp.float32)
                + part[half, index, :, own].astype(jnp.float32)
                + down_in[half, index, :, own].astype(jnp.float32)
            ).astype(LOW)
            grad_hidden[...] = jnp.concatenate([both[0], both[1]], axis=1)

    @pl.when(step == steps - 1)
    def _():
        for side in range(2):
            for owner in range(n):
                pltpu.make_async_copy(
                    text.at[side, owner],
                    grad_text.at[pl.ds(owner * block + side * sub, sub)],
                    text_sem.at[side, owner],
                ).wait()


def shards(
    queries,
    keys,
    values,
    grad_attention,
    normed,
    norm_scale,
    norm_gain,
    key_weight,
    value_weight,
    key_down,
    key_up,
    value_down,
    value_up,
    out_weight,
):
    rows, columns = queries.shape[1:]
    length, features = normed.shape[1:]
    rank = key_up.shape[0]
    hidden = out_weight.shape[0]
    n, splits, prompts = lax.axis_size("seq"), lax.axis_size("tp"), lax.axis_size("dp")
    heads = columns // HD
    width = 2 * HD
    slices = hidden // width
    lag = 2 * (n - 1)
    first = max(2 * heads, heads + lag + 6)
    second = max(first + slices, 2 * heads + lag + 6)
    steps = max(second + slices + lag, 2 * heads + lag + 14)
    block = length // n
    sub = block // 2
    half_length = length // 2
    share = 2 * rank // n
    plan = dict(
        n=n,
        splits=splits,
        prompts=prompts,
        heads=heads,
        slices=slices,
        lag=lag,
        first=first,
        second=second,
        steps=steps,
        features_whole=features * n,
    )

    def early(height):
        return pl.BlockSpec((height, HD), lambda step: (0, jnp.minimum(step, heads - 1)))

    def late(height):
        def place(step):
            at = jnp.clip(step - lag, 0, 2 * heads - 1)
            return 0, at - jnp.where(at >= heads, heads, 0)

        return pl.BlockSpec((height, HD), place)

    def fixed(height, size):
        return pl.BlockSpec((height, size), lambda step: (0, 0))

    def slice_of(step):
        after = step >= second
        return after.astype(jnp.int32), jnp.clip(
            step - jnp.where(after, second, first), 0, slices - 1
        )

    buffer = pltpu.VMEM((2, max(heads, slices), 2, half_length, HD), LOW)
    dma = pltpu.SemaphoreType.DMA
    grad_query, grad_hidden, grad_text, down_key, down_value, up_key, up_value = pl.pallas_call(
        functools.partial(kernel, plan),
        grid=(steps,),
        out_shape=(
            jax.ShapeDtypeStruct((rows, columns), LOW),
            jax.ShapeDtypeStruct((block, hidden), LOW),
            jax.ShapeDtypeStruct((length, features), LOW),
            jax.ShapeDtypeStruct((rank, features), jnp.float32),
            jax.ShapeDtypeStruct((rank, features), jnp.float32),
            jax.ShapeDtypeStruct((rank, columns), jnp.float32),
            jax.ShapeDtypeStruct((rank, columns), jnp.float32),
        ),
        in_specs=[
            early(rows),
            early(length),
            early(length),
            early(rows),
            late(features),
            late(features),
            late(rank),
            late(rank),
            pl.BlockSpec((width, features), lambda step: (slice_of(step)[1], 0)),
            fixed(length, features),
            fixed(1, length),
            fixed(1, features),
            fixed(rank, features),
            fixed(rank, features),
        ],
        out_specs=(
            early(rows),
            pl.BlockSpec((sub, width), lambda step: slice_of(step - lag)),
            pl.BlockSpec(memory_space=pl.ANY),
            fixed(rank, features),
            fixed(rank, features),
            fixed(rank, columns),
            fixed(rank, columns),
        ),
        scratch_shapes=[buffer] * 5
        + [
            pltpu.VMEM((2, half_length, features), jnp.float32),
            pltpu.VMEM((2, half_length, 2 * rank), jnp.float32),
            pltpu.VMEM((2, splits, half_length, features), LOW),
            pltpu.VMEM((2, splits, half_length, 2 * rank), LOW),
            pltpu.VMEM((2, n, sub, features), LOW),
            pltpu.VMEM((2, n, 8, half_length), jnp.float32),
            pltpu.VMEM((n, share, length), LOW),
            pltpu.VMEM((n, share, length), LOW),
            pltpu.VMEM((2, share, half_length), LOW),
            pltpu.VMEM((heads, share, HD), jnp.float32),
            pltpu.VMEM((prompts, share, columns), LOW),
            pltpu.VMEM((n, share, columns), LOW),
            pltpu.VMEM((2 * rank, features), jnp.float32),
            pltpu.VMEM((prompts, 2 * rank, features), LOW),
        ]
        + [dma((2, heads))] * 4
        + [dma((2, slices))] * 4
        + [dma((2, splits))] * 4
        + [dma((2, n))] * 2
        + [dma((n,))] * 2
        + [dma((prompts,))] * 4
        + [dma((n,))] * 2
        + [dma((2, n))],
        compiler_params=pltpu.CompilerParams(
            collective_id=0, has_side_effects=True, vmem_limit_bytes=62 * 1024 * 1024
        ),
        name="fused",
    )(
        queries[0],
        keys[0],
        values[0],
        grad_attention[0],
        key_weight,
        value_weight,
        key_up,
        value_up,
        out_weight,
        normed[0],
        norm_scale,
        norm_gain[None, :],
        key_down.T,
        value_down.T,
    )
    return (
        grad_query[None],
        grad_text[None],
        grad_hidden[None],
        down_key.T,
        up_key,
        down_value.T,
        up_value,
    )


def solution(mesh):
    return jax.shard_map(
        shards,
        mesh=mesh,
        in_specs=(
            P("dp", "seq", "tp"),
            P("dp", None, "tp"),
            P("dp", None, "tp"),
            P("dp", "seq", "tp"),
            P("dp", None, "seq"),
            P("dp", None),
            P("seq"),
            P("seq", "tp"),
            P("seq", "tp"),
            P("seq", None),
            P(None, "tp"),
            P("seq", None),
            P(None, "tp"),
            P("tp", "seq"),
        ),
        out_specs=(
            P("dp", "seq", "tp"),
            P("dp", None, "seq"),
            P("dp", "seq", "tp"),
            P("seq", None),
            P(None, "tp"),
            P("seq", None),
            P(None, "tp"),
        ),
        check_vma=False,
    )
```

```python
import functools

import jax
import jax.numpy as jnp
from jax import lax
from jax.experimental import pallas as pl
from jax.experimental.pallas import tpu as pltpu
from jax.sharding import PartitionSpec as P

HD = 128
MESH = pl.DeviceIdType.MESH
LOW = jnp.bfloat16


def dot(left_side, right_side, left_dim, right_dim):
    return lax.dot_general(
        left_side,
        right_side,
        (((left_dim,), (right_dim,)), ((), ())),
        preferred_element_type=jnp.float32,
    )


def exchange(axis, size, landing, send, recv):
    me = lax.axis_index(axis)

    def copy(slot, offset):
        return pltpu.make_async_remote_copy(
            src_ref=landing.at[slot],
            dst_ref=landing.at[slot],
            send_sem=send.at[offset],
            recv_sem=recv.at[slot],
            device_id={axis: lax.rem(me + offset, size)},
            device_id_type=MESH,
        )

    def start():
        for offset in range(1, size):
            copy(me, offset).start()

    def finish():
        for offset in range(1, size):
            copy(lax.rem(me + offset, size), offset).wait_recv()
        for offset in range(1, size):
            copy(me, offset).wait_send()

    return start, finish


def low_sum(ref, size):
    value = ref[0].astype(jnp.float32)
    for index in range(1, size):
        value = value + ref[index].astype(jnp.float32)
    return value


def kernel(
    plan,
    queries,
    keys,
    values,
    grads,
    key_weight,
    value_weight,
    key_up,
    value_up,
    out_weight,
    normed,
    scale,
    gain,
    key_down,
    value_down,
    grad_query,
    grad_hidden,
    grad_text,
    key_down_grad,
    value_down_grad,
    key_up_grad,
    value_up_grad,
    part,
    up_in,
    up_out,
    down_in,
    down_out,
    total,
    project,
    context_all,
    project_all,
    text,
    sum_all,
    latent_own,
    latent_all,
    latent,
    up_sum,
    up_own,
    up_all,
    rows_all,
    up_whole,
    down_sum,
    down_all,
    up_send,
    up_recv,
    down_send,
    down_recv,
    high_send,
    high_recv,
    low_send,
    low_recv,
    context_send,
    context_recv,
    project_send,
    project_recv,
    sum_send,
    sum_recv,
    latent_send,
    latent_recv,
    up_dp_send,
    up_dp_recv,
    down_dp_send,
    down_dp_recv,
    rows_send,
    rows_recv,
    whole_send,
    whole_recv,
    near_up_send,
    near_up_recv,
    near_down_send,
    near_down_recv,
    text_sem,
):
    n, splits, prompts = plan["n"], plan["splits"], plan["prompts"]
    heads, slices, lag = plan["heads"], plan["slices"], plan["lag"]
    first, second, steps = plan["first"], plan["second"], plan["steps"]
    length, features = normed.shape
    block = length // n
    sub = block // 2
    half_length = length // 2
    rank = key_down.shape[0]
    step = pl.program_id(0)
    me = lax.axis_index("seq")
    split = lax.axis_index("tp")
    prompt = lax.axis_index("dp")
    factor = HD ** (-0.5)
    above = lax.rem(me + 1, n)
    below = lax.rem(me + n - 1, n)
    has_low = me > 0
    has_high = me < n - 1

    def rows_of(value, half):
        return jnp.concatenate(
            [
                value[owner * block + half * sub : owner * block + half * sub + sub]
                for owner in range(n)
            ],
            axis=0,
        )

    def context_of(half):
        return (rows_of(normed, half).astype(jnp.float32) * gain[...]).astype(LOW)

    def column(row, size):
        return jnp.transpose(jnp.broadcast_to(row, (128, size)))[:, :1]

    def up_copy(half, index, source):
        return pltpu.make_async_remote_copy(
            src_ref=source.at[half, index],
            dst_ref=up_in.at[half, index],
            send_sem=up_send.at[half, index],
            recv_sem=up_recv.at[half, index],
            device_id={"seq": above},
            device_id_type=MESH,
        )

    def down_copy(half, index, source):
        return pltpu.make_async_remote_copy(
            src_ref=source.at[half, index],
            dst_ref=down_in.at[half, index],
            send_sem=down_send.at[half, index],
            recv_sem=down_recv.at[half, index],
            device_id={"seq": below},
            device_id_type=MESH,
        )

    def high_copy(half, index, source, owner):
        rows = pl.ds(owner * sub, (n - owner) * sub)
        return pltpu.make_async_remote_copy(
            src_ref=source.at[half, index, :, rows],
            dst_ref=up_in.at[half, index, :, rows],
            send_sem=high_send.at[half, index],
            recv_sem=high_recv.at[half, index],
            device_id={"seq": above},
            device_id_type=MESH,
        )

    def low_copy(half, index, source, owner):
        rows = pl.ds(0, (owner + 1) * sub)
        return pltpu.make_async_remote_copy(
            src_ref=source.at[half, index, :, rows],
            dst_ref=down_in.at[half, index, :, rows],
            send_sem=low_send.at[half, index],
            recv_sem=low_recv.at[half, index],
            device_id={"seq": below},
            device_id_type=MESH,
        )

    def near_up_copy(half, index):
        rows = pl.ds(sub, sub)
        return pltpu.make_async_remote_copy(
            src_ref=part.at[half, index, :, rows],
            dst_ref=up_in.at[half, index, :, rows],
            send_sem=near_up_send.at[half, index],
            recv_sem=near_up_recv.at[half, index],
            device_id={"seq": above},
            device_id_type=MESH,
        )

    def near_down_copy(half, index):
        rows = pl.ds((n - 2) * sub, sub)
        return pltpu.make_async_remote_copy(
            src_ref=part.at[half, index, :, rows],
            dst_ref=down_in.at[half, index, :, rows],
            send_sem=near_down_send.at[half, index],
            recv_sem=near_down_recv.at[half, index],
            device_id={"seq": below},
            device_id_type=MESH,
        )

    def attend(position):
        live = jnp.logical_and(position >= 0, position < 2 * heads)
        half = (position >= heads).astype(jnp.int32)
        return live, half, position - half * heads

    def hide(position):
        live = jnp.logical_or(
            jnp.logical_and(position >= first, position < first + slices),
            jnp.logical_and(position >= second, position < second + slices),
        )
        half = (position >= second).astype(jnp.int32)
        return live, half, position - first - half * (second - first)

    @pl.when(step == 0)
    def _():
        barrier = pltpu.get_barrier_semaphore()
        for axis, size in (("tp", splits), ("seq", n), ("dp", prompts)):
            for offset in range(1, size):
                pl.semaphore_signal(
                    barrier,
                    inc=1,
                    device_id={axis: lax.rem(lax.axis_index(axis) + offset, size)},
                    device_id_type=MESH,
                )

    @pl.when(step < heads)
    def _():
        query, key, value, grad = queries[...], keys[...], values[...], grads[...]
        scores = dot(key, query, 1, 1) * factor
        weights = jnp.exp(scores - jnp.max(scores, axis=0, keepdims=True))
        probability = weights * (1.0 / jnp.sum(weights, axis=0, keepdims=True))
        value_part = dot(probability.astype(LOW), grad, 1, 0).astype(LOW)
        grad_probs = dot(value, grad, 1, 1)
        grad_scores = probability * (
            grad_probs - jnp.sum(probability * grad_probs, axis=0, keepdims=True)
        )
        grad_low = grad_scores.astype(LOW)
        key_part = (dot(grad_low, query, 1, 0) * factor).astype(LOW)
        for kind, side in ((0, key_part), (1, value_part)):
            for half in range(2):
                part[half, step, kind] = rows_of(side, half)
        grad_query[...] = (dot(grad_low, key, 0, 0) * factor).astype(LOW)

    @pl.when(step == 0)
    def _():
        pl.semaphore_wait(pltpu.get_barrier_semaphore(), splits + n + prompts - 3)

    live, half, index = hide(step)

    @pl.when(live)
    def _():
        product = dot(text[half].reshape(half_length, features), out_weight[...], 1, 1)
        product = product.astype(LOW)
        part[half, index, 0] = product[:, :HD]
        part[half, index, 1] = product[:, HD:]

    up_at = step - 2 * me
    down_at = step - 2 * (n - 1 - me)

    live, half, index = attend(up_at)

    @pl.when(jnp.logical_and(live, me == 0))
    def _():
        up_copy(half, index, part).start()
        up_in[half, index] = jnp.zeros(up_in.shape[2:], LOW)

    @pl.when(jnp.logical_and(live, has_low))
    def _():
        up_copy(half, index, up_out).wait_recv()

        @pl.when(has_high)
        def _():
            up_out[half, index] = up_in[half, index] + part[half, index]
            up_copy(half, index, up_out).start()

    live, half, index = attend(down_at)

    @pl.when(jnp.logical_and(live, me == n - 1))
    def _():
        down_copy(half, index, part).start()
        down_in[half, index] = jnp.zeros(down_in.shape[2:], LOW)

    @pl.when(jnp.logical_and(live, has_high))
    def _():
        down_copy(half, index, down_out).wait_recv()

        @pl.when(has_low)
        def _():
            down_out[half, index] = down_in[half, index] + part[half, index]
            down_copy(half, index, down_out).start()

    live, half, index = hide(up_at)
    for place in range(n):

        @pl.when(jnp.logical_and(live, me == place))
        def _():
            if place == 0:
                up_in[half, index, :, :sub] = jnp.zeros((2, sub, HD), LOW)
                if n > 2:
                    high_copy(half, index, part, 2).start()
            elif place == 1:
                if n > 2:
                    high_copy(half, index, up_out, 2).wait_recv()
            else:
                high_copy(half, index, up_out, place).wait_recv()
            if 0 < place < n - 1:
                rest = (place + 1) * sub
                up_out[half, index, :, rest:] = (
                    up_in[half, index, :, rest:] + part[half, index, :, rest:]
                )
                high_copy(half, index, up_out, place + 1).start()

    live, half, index = hide(down_at)
    for place in range(n):

        @pl.when(jnp.logical_and(live, me == place))
        def _():
            if place == n - 1:
                down_in[half, index, :, place * sub :] = jnp.zeros((2, sub, HD), LOW)
                if n > 2:
                    low_copy(half, index, part, n - 3).start()
            elif place == n - 2:
                if n > 2:
                    low_copy(half, index, down_out, n - 3).wait_recv()
            else:
                low_copy(half, index, down_out, place).wait_recv()
            if 0 < place < n - 1:
                rest = place * sub
                down_out[half, index, :, :rest] = (
                    down_in[half, index, :, :rest] + part[half, index, :, :rest]
                )
                low_copy(half, index, down_out, place - 1).start()

    live, half, index = hide(step - plan["delay"])

    @pl.when(jnp.logical_and(live, me == 0))
    def _():
        near_up_copy(half, index).start()

    @pl.when(jnp.logical_and(live, me == n - 1))
    def _():
        near_down_copy(half, index).start()

    @pl.when(step == 0)
    def _():
        total[...] = jnp.zeros_like(total)
        project[...] = jnp.zeros_like(project)
        up_sum[...] = jnp.zeros_like(up_sum)

    def latent_copy(slot, owner, offset):
        return pltpu.make_async_remote_copy(
            src_ref=latent_own.at[owner],
            dst_ref=latent_all.at[slot],
            send_sem=latent_send.at[offset],
            recv_sem=latent_recv.at[slot],
            device_id={"seq": lax.rem(me + offset, n)},
            device_id_type=MESH,
        )

    @pl.when(step == 1)
    def _():
        down = jnp.concatenate([key_down[...], value_down[...]], axis=0)
        sides = [dot(down, context_of(side), 1, 1) for side in range(2)]
        latent_own[...] = (
            jnp.concatenate(sides, axis=1).reshape(latent_own.shape).astype(LOW)
        )
        for offset in range(1, n):
            latent_copy(me, lax.rem(me + offset, n), offset).start()
        latent_all[me] = latent_own[me]

    @pl.when(step == lag - 1)
    def _():
        for offset in range(1, n):
            latent_copy(lax.rem(me + offset, n), me, offset).wait_recv()
        for offset in range(1, n):
            latent_copy(me, lax.rem(me + offset, n), offset).wait_send()
        both = low_sum(latent_all, n).astype(LOW)
        for side in range(2):
            latent[side] = both[:, side * half_length : (side + 1) * half_length]

    live, half, index = attend(step - lag)

    @pl.when(live)
    def _():
        @pl.when(has_high)
        def _():
            up_copy(half, index, up_out).wait_send()

        @pl.when(has_low)
        def _():
            down_copy(half, index, down_out).wait_send()

        both = (
            up_in[half, index].astype(jnp.float32)
            + part[half, index].astype(jnp.float32)
            + down_in[half, index].astype(jnp.float32)
        ).astype(LOW)
        pair = jnp.concatenate([both[0], both[1]], axis=1)
        slab = jnp.concatenate([key_weight[...], value_weight[...]], axis=1)
        total[half] += dot(pair, slab, 1, 1)
        blank = jnp.zeros((rank, HD), LOW)
        rises = jnp.concatenate(
            [
                jnp.concatenate([key_up[...], blank], axis=1),
                jnp.concatenate([blank, value_up[...]], axis=1),
            ],
            axis=0,
        )
        project[half] += dot(pair, rises, 1, 1)
        own = jnp.where(me < n // 2, both[0], both[1])
        up_sum[index] += dot(latent[half], own, 1, 0)

    for side in range(2):
        end = heads * (side + 1) + lag - 1
        project_start, project_finish = exchange(
            "tp", splits, project_all.at[side], project_send.at[side], project_recv.at[side]
        )
        context_start, context_finish = exchange(
            "tp", splits, context_all.at[side], context_send.at[side], context_recv.at[side]
        )
        sum_start, sum_finish = exchange(
            "seq", n, sum_all.at[side], sum_send.at[side], sum_recv.at[side]
        )

        @pl.when(step == end)
        def _():
            project_all[side, split] = project[side].astype(LOW)
            context_all[side, split] = total[side].astype(LOW)
            project_start()
            context_start()

        @pl.when(step == end + 2)
        def _():
            project_finish()
            context_finish()
            back = low_sum(project_all.at[side], splits).astype(LOW)
            low_rank = dot(back[:, :rank], key_down[...], 1, 0) + dot(
                back[:, rank:], value_down[...], 1, 0
            )
            scaled = gain[...] * (low_sum(context_all.at[side], splits) + low_rank)
            total[side] = scaled
            local_sum = jnp.sum(
                rows_of(normed, side).astype(jnp.float32) * scaled, axis=1, keepdims=True
            )
            line = jnp.transpose(jnp.broadcast_to(local_sum, (half_length, 128)))[:1, :]
            sum_all[side, me] = jnp.concatenate(
                [line[:, at : at + 128] for at in range(0, half_length, 128)], axis=0
            )
            sum_start()
            down = dot(back, context_of(side), 0, 0)
            if side == 0:
                down_sum[...] = down
            else:
                down_sum[...] += down

        @pl.when(step == end + 6)
        def _():
            sum_finish()
            token_sum = sum_all[side, 0]
            for other in range(1, n):
                token_sum = token_sum + sum_all[side, other]
            line = jnp.concatenate(
                [token_sum[at : at + 1] for at in range(half_length // 128)], axis=1
            )
            token_column = column(line, half_length)
            result = rows_of(column(scale[...], length), side) * (
                total[side]
                - rows_of(normed, side).astype(jnp.float32)
                * (token_column / plan["features_whole"])
            )
            text[side] = result.astype(LOW).reshape(n, sub, features)
            for owner in range(n):
                pltpu.make_async_copy(
                    text.at[side, owner],
                    grad_text.at[pl.ds(owner * block + side * sub, sub)],
                    text_sem.at[side, owner],
                ).start()

    end = 2 * heads + lag - 1
    portion = up_own.shape[2]

    def up_piece(slot, owner, offset):
        return pltpu.make_async_remote_copy(
            src_ref=up_own.at[owner],
            dst_ref=up_all.at[slot],
            send_sem=up_dp_send.at[offset],
            recv_sem=up_dp_recv.at[slot],
            device_id={"dp": lax.rem(prompt + offset, prompts)},
            device_id_type=MESH,
        )

    whole_start, whole_finish = exchange("dp", prompts, up_whole, whole_send, whole_recv)
    down_start, down_finish = exchange("dp", prompts, down_all, down_dp_send, down_dp_recv)
    rows_start, rows_finish = exchange("seq", n, rows_all, rows_send, rows_recv)

    @pl.when(step == end + 1)
    def _():
        rows = jnp.concatenate([up_sum[index] for index in range(heads)], axis=1).astype(LOW)
        for owner in range(prompts):
            up_own[owner] = rows[:, owner * portion : (owner + 1) * portion]
        for offset in range(1, prompts):
            up_piece(prompt, lax.rem(prompt + offset, prompts), offset).start()
        up_all[prompt] = up_own[prompt]

    @pl.when(step == end + 3)
    def _():
        down_all[prompt] = down_sum[...].astype(LOW)
        down_start()

    @pl.when(step == end + 5)
    def _():
        for offset in range(1, prompts):
            up_piece(lax.rem(prompt + offset, prompts), prompt, offset).wait_recv()
        for offset in range(1, prompts):
            up_piece(prompt, lax.rem(prompt + offset, prompts), offset).wait_send()
        rows_all[me] = (low_sum(up_all, prompts) / prompts).astype(LOW)
        rows_start()

    @pl.when(step == end + 9)
    def _():
        down_finish()
        down = low_sum(down_all, prompts)
        key_down_grad[...] = down[:rank] / prompts
        value_down_grad[...] = down[rank:] / prompts

    @pl.when(step == end + 12)
    def _():
        rows_finish()
        up_whole[prompt] = rows_all[...]
        whole_start()

    @pl.when(step == end + 18)
    def _():
        whole_finish()
        for owner in range(prompts):
            columns = slice(owner * portion, (owner + 1) * portion)
            rows = up_whole[owner].astype(jnp.float32).reshape(2 * rank, portion)
            key_up_grad[:, columns] = rows[:rank]
            value_up_grad[:, columns] = rows[rank:]

    live, half, index = hide(step - lag)
    for place in range(n):

        @pl.when(jnp.logical_and(live, me == place))
        def _():
            if place == 0:
                near_up_copy(half, index).wait_send()
            if place == 1:
                near_up_copy(half, index).wait_recv()
            if place == n - 2:
                near_down_copy(half, index).wait_recv()
            if place == n - 1:
                near_down_copy(half, index).wait_send()
            if place < n - 1 and n > 2:
                high_copy(half, index, up_out, max(place + 1, 2)).wait_send()
            if place > 0 and n > 2:
                low_copy(half, index, down_out, min(place - 1, n - 3)).wait_send()
            own = slice(place * sub, (place + 1) * sub)
            both = (
                up_in[half, index, :, own].astype(jnp.float32)
                + part[half, index, :, own].astype(jnp.float32)
                + down_in[half, index, :, own].astype(jnp.float32)
            ).astype(LOW)
            grad_hidden[...] = jnp.concatenate([both[0], both[1]], axis=1)

    @pl.when(step == steps - 1)
    def _():
        for side in range(2):
            for owner in range(n):
                pltpu.make_async_copy(
                    text.at[side, owner],
                    grad_text.at[pl.ds(owner * block + side * sub, sub)],
                    text_sem.at[side, owner],
                ).wait()


def store_kernel(count, pieces, *refs):
    sources, results, stages = refs[:count], refs[count : 2 * count], refs[2 * count : 3 * count]
    load_sem, store_sem = refs[3 * count :]

    def copies(item, piece):
        rows = sources[item].shape[0] // pieces[item]
        at = pl.ds(piece * rows, rows)
        slot = sum(pieces[:item]) + piece
        return (
            pltpu.make_async_copy(
                sources[item].at[at], stages[item].at[at], load_sem.at[slot]
            ),
            pltpu.make_async_copy(
                stages[item].at[at], results[item].at[at], store_sem.at[slot]
            ),
        )

    every = [copies(item, piece) for item in range(count) for piece in range(pieces[item])]
    for load, _ in every:
        load.start()
    for load, store in every:
        load.wait()
        store.start()
    for _, store in every:
        store.wait()


def store(*arrays):
    pieces = [
        4 if value.shape[0] % 64 == 0 and value.size >= 2**18 else 1 for value in arrays
    ]
    total = sum(pieces)
    anywhere = pl.BlockSpec(memory_space=pl.ANY)
    return pl.pallas_call(
        functools.partial(store_kernel, len(arrays), pieces),
        out_shape=tuple(jax.ShapeDtypeStruct(value.shape, value.dtype) for value in arrays),
        in_specs=[anywhere] * len(arrays),
        out_specs=(anywhere,) * len(arrays),
        scratch_shapes=[pltpu.VMEM(value.shape, value.dtype) for value in arrays]
        + [pltpu.SemaphoreType.DMA((total,))] * 2,
        name="store",
    )(*arrays)


def shards(
    queries,
    keys,
    values,
    grad_attention,
    normed,
    norm_scale,
    norm_gain,
    key_weight,
    value_weight,
    key_down,
    key_up,
    value_down,
    value_up,
    out_weight,
):
    rows, columns = queries.shape[1:]
    length, features = normed.shape[1:]
    rank = key_up.shape[0]
    hidden = out_weight.shape[0]
    n, splits, prompts = lax.axis_size("seq"), lax.axis_size("tp"), lax.axis_size("dp")
    heads = columns // HD
    width = 2 * HD
    slices = hidden // width
    lag = 2 * (n - 1)
    first = max(2 * heads, heads + lag + 6)
    second = max(first + slices, 2 * heads + lag + 6)
    steps = max(second + slices + lag, 2 * heads + lag + 18)
    block = length // n
    sub = block // 2
    half_length = length // 2
    share = 2 * rank // n
    plan = dict(
        n=n,
        splits=splits,
        prompts=prompts,
        heads=heads,
        slices=slices,
        lag=lag,
        delay=max(0, min(4, lag - 2)),
        first=first,
        second=second,
        steps=steps,
        features_whole=features * n,
    )

    def early(height):
        return pl.BlockSpec((height, HD), lambda step: (0, jnp.minimum(step, heads - 1)))

    def late(height):
        def place(step):
            at = jnp.clip(step - lag, 0, 2 * heads - 1)
            return 0, at - jnp.where(at >= heads, heads, 0)

        return pl.BlockSpec((height, HD), place)

    def fixed(height, size):
        return pl.BlockSpec((height, size), lambda step: (0, 0))

    def slice_of(step):
        after = step >= second
        return after.astype(jnp.int32), jnp.clip(
            step - jnp.where(after, second, first), 0, slices - 1
        )

    buffer = pltpu.VMEM((2, max(heads, slices), 2, half_length, HD), LOW)
    dma = pltpu.SemaphoreType.DMA
    grad_query, grad_hidden, grad_text, down_key, down_value, up_key, up_value = pl.pallas_call(
        functools.partial(kernel, plan),
        grid=(steps,),
        out_shape=(
            jax.ShapeDtypeStruct((rows, columns), LOW),
            jax.ShapeDtypeStruct((block, hidden), LOW),
            jax.ShapeDtypeStruct((length, features), LOW),
            jax.ShapeDtypeStruct((rank, features), jnp.float32),
            jax.ShapeDtypeStruct((rank, features), jnp.float32),
            jax.ShapeDtypeStruct((rank, columns), jnp.float32),
            jax.ShapeDtypeStruct((rank, columns), jnp.float32),
        ),
        in_specs=[
            early(rows),
            early(length),
            early(length),
            early(rows),
            late(features),
            late(features),
            late(rank),
            late(rank),
            pl.BlockSpec((width, features), lambda step: (slice_of(step)[1], 0)),
            fixed(length, features),
            fixed(1, length),
            fixed(1, features),
            fixed(rank, features),
            fixed(rank, features),
        ],
        out_specs=(
            early(rows),
            pl.BlockSpec((sub, width), lambda step: slice_of(step - lag)),
            pl.BlockSpec(memory_space=pl.ANY),
            fixed(rank, features),
            fixed(rank, features),
            fixed(rank, columns),
            fixed(rank, columns),
        ),
        scratch_shapes=[buffer] * 5
        + [
            pltpu.VMEM((2, half_length, features), jnp.float32),
            pltpu.VMEM((2, half_length, 2 * rank), jnp.float32),
            pltpu.VMEM((2, splits, half_length, features), LOW),
            pltpu.VMEM((2, splits, half_length, 2 * rank), LOW),
            pltpu.VMEM((2, n, sub, features), LOW),
            pltpu.VMEM((2, n, half_length // 128, 128), jnp.float32),
            pltpu.VMEM((n, share, length), LOW),
            pltpu.VMEM((n, share, length), LOW),
            pltpu.VMEM((2, share, half_length), LOW),
            pltpu.VMEM((heads, share, HD), jnp.float32),
            pltpu.VMEM((prompts, share, columns // prompts), LOW),
            pltpu.VMEM((prompts, share, columns // prompts), LOW),
            pltpu.VMEM((n, share, columns // prompts), LOW),
            pltpu.VMEM((prompts, n, share, columns // prompts), LOW),
            pltpu.VMEM((2 * rank, features), jnp.float32),
            pltpu.VMEM((prompts, 2 * rank, features), LOW),
        ]
        + [dma((2, heads))] * 4
        + [dma((2, slices))] * 4
        + [dma((2, splits))] * 4
        + [dma((2, n))] * 2
        + [dma((n,))] * 2
        + [dma((prompts,))] * 4
        + [dma((n,))] * 2
        + [dma((prompts,))] * 2
        + [dma((2, slices))] * 4
        + [dma((2, n))],
        compiler_params=pltpu.CompilerParams(
            collective_id=0, has_side_effects=True, vmem_limit_bytes=62 * 1024 * 1024
        ),
        name="fused",
    )(
        queries[0],
        keys[0],
        values[0],
        grad_attention[0],
        key_weight,
        value_weight,
        key_up,
        value_up,
        out_weight,
        normed[0],
        norm_scale,
        norm_gain[None, :],
        key_down.T,
        value_down.T,
    )
    grad_query, grad_hidden, grad_text, down_key, down_value, up_key, up_value = store(
        grad_query, grad_hidden, grad_text, down_key, down_value, up_key, up_value
    )
    return (
        grad_query[None],
        grad_text[None],
        grad_hidden[None],
        down_key.T,
        up_key,
        down_value.T,
        up_value,
    )


def solution(mesh):
    return jax.shard_map(
        shards,
        mesh=mesh,
        in_specs=(
            P("dp", "seq", "tp"),
            P("dp", None, "tp"),
            P("dp", None, "tp"),
            P("dp", "seq", "tp"),
            P("dp", None, "seq"),
            P("dp", None),
            P("seq"),
            P("seq", "tp"),
            P("seq", "tp"),
            P("seq", None),
            P(None, "tp"),
            P("seq", None),
            P(None, "tp"),
            P("tp", "seq"),
        ),
        out_specs=(
            P("dp", "seq", "tp"),
            P("dp", None, "seq"),
            P("dp", "seq", "tp"),
            P("seq", None),
            P(None, "tp"),
            P("seq", None),
            P(None, "tp"),
        ),
        check_vma=False,
    )
```

```python
import functools

import jax
import jax.numpy as jnp
from jax import lax
from jax.experimental import pallas as pl
from jax.experimental.pallas import tpu as pltpu
from jax.sharding import PartitionSpec as P

HD = 128
MESH = pl.DeviceIdType.MESH
LOW = jnp.bfloat16


def dot(left_side, right_side, left_dim, right_dim):
    return lax.dot_general(
        left_side,
        right_side,
        (((left_dim,), (right_dim,)), ((), ())),
        preferred_element_type=jnp.float32,
    )


def exchange(axis, size, landing, send, recv):
    me = lax.axis_index(axis)

    def copy(slot, offset):
        return pltpu.make_async_remote_copy(
            src_ref=landing.at[slot],
            dst_ref=landing.at[slot],
            send_sem=send.at[offset],
            recv_sem=recv.at[slot],
            device_id={axis: lax.rem(me + offset, size)},
            device_id_type=MESH,
        )

    def start():
        for offset in range(1, size):
            copy(me, offset).start()

    def finish():
        for offset in range(1, size):
            copy(lax.rem(me + offset, size), offset).wait_recv()
        for offset in range(1, size):
            copy(me, offset).wait_send()

    return start, finish


def low_sum(ref, size):
    value = ref[0].astype(jnp.float32)
    for index in range(1, size):
        value = value + ref[index].astype(jnp.float32)
    return value


def kernel(
    plan,
    queries,
    keys,
    values,
    grads,
    key_weight,
    value_weight,
    key_up,
    value_up,
    out_weight,
    normed,
    scale,
    gain,
    key_down,
    value_down,
    grad_query,
    grad_hidden,
    grad_text,
    key_down_grad,
    value_down_grad,
    key_up_grad,
    value_up_grad,
    part,
    up_in,
    up_out,
    down_in,
    down_out,
    total,
    project,
    context_all,
    project_all,
    text,
    sum_all,
    latent_own,
    latent_all,
    latent,
    up_sum,
    up_own,
    up_all,
    rows_all,
    up_whole,
    down_sum,
    down_all,
    up_send,
    up_recv,
    down_send,
    down_recv,
    context_send,
    context_recv,
    project_send,
    project_recv,
    sum_send,
    sum_recv,
    latent_send,
    latent_recv,
    up_dp_send,
    up_dp_recv,
    down_dp_send,
    down_dp_recv,
    rows_send,
    rows_recv,
    whole_send,
    whole_recv,
    near_up_send,
    near_up_recv,
    near_down_send,
    near_down_recv,
    text_sem,
):
    n, splits, prompts = plan["n"], plan["splits"], plan["prompts"]
    heads, slices, lag = plan["heads"], plan["slices"], plan["lag"]
    first, second, steps = plan["first"], plan["second"], plan["steps"]
    length, features = normed.shape
    block = length // n
    sub = block // 2
    half_length = length // 2
    rank = key_down.shape[0]
    step = pl.program_id(0)
    me = lax.axis_index("seq")
    split = lax.axis_index("tp")
    prompt = lax.axis_index("dp")
    factor = HD ** (-0.5)
    above = lax.rem(me + 1, n)
    below = lax.rem(me + n - 1, n)
    has_low = me > 0
    has_high = me < n - 1

    def rows_of(value, half):
        return jnp.concatenate(
            [
                value[owner * block + half * sub : owner * block + half * sub + sub]
                for owner in range(n)
            ],
            axis=0,
        )

    def context_of(half):
        return (rows_of(normed, half).astype(jnp.float32) * gain[...]).astype(LOW)

    def column(row, size):
        return jnp.transpose(jnp.broadcast_to(row, (128, size)))[:, :1]

    ring = plan["ring"]

    def heads_ring(half, index):
        return lax.rem(index + half * heads, ring)

    def hidden_ring(half, index):
        return lax.rem(first + index + half * (second - first), ring)

    def up_copy(half, index, source):
        return pltpu.make_async_remote_copy(
            src_ref=source.at[half, index],
            dst_ref=up_in.at[half, index],
            send_sem=up_send.at[heads_ring(half, index)],
            recv_sem=up_recv.at[heads_ring(half, index)],
            device_id={"seq": above},
            device_id_type=MESH,
        )

    def down_copy(half, index, source):
        return pltpu.make_async_remote_copy(
            src_ref=source.at[half, index],
            dst_ref=down_in.at[half, index],
            send_sem=down_send.at[heads_ring(half, index)],
            recv_sem=down_recv.at[heads_ring(half, index)],
            device_id={"seq": below},
            device_id_type=MESH,
        )

    def high_copy(half, index, source, owner):
        rows = pl.ds(owner * sub, (n - owner) * sub)
        return pltpu.make_async_remote_copy(
            src_ref=source.at[half, index, :, rows],
            dst_ref=up_in.at[half, index, :, rows],
            send_sem=up_send.at[hidden_ring(half, index)],
            recv_sem=up_recv.at[hidden_ring(half, index)],
            device_id={"seq": above},
            device_id_type=MESH,
        )

    def low_copy(half, index, source, owner):
        rows = pl.ds(0, (owner + 1) * sub)
        return pltpu.make_async_remote_copy(
            src_ref=source.at[half, index, :, rows],
            dst_ref=down_in.at[half, index, :, rows],
            send_sem=down_send.at[hidden_ring(half, index)],
            recv_sem=down_recv.at[hidden_ring(half, index)],
            device_id={"seq": below},
            device_id_type=MESH,
        )

    def near_up_copy(half, index):
        rows = pl.ds(sub, sub)
        return pltpu.make_async_remote_copy(
            src_ref=part.at[half, index, :, rows],
            dst_ref=up_in.at[half, index, :, rows],
            send_sem=near_up_send.at[hidden_ring(half, index)],
            recv_sem=near_up_recv.at[hidden_ring(half, index)],
            device_id={"seq": above},
            device_id_type=MESH,
        )

    def near_down_copy(half, index):
        rows = pl.ds((n - 2) * sub, sub)
        return pltpu.make_async_remote_copy(
            src_ref=part.at[half, index, :, rows],
            dst_ref=down_in.at[half, index, :, rows],
            send_sem=near_down_send.at[hidden_ring(half, index)],
            recv_sem=near_down_recv.at[hidden_ring(half, index)],
            device_id={"seq": below},
            device_id_type=MESH,
        )

    def attend(position):
        live = jnp.logical_and(position >= 0, position < 2 * heads)
        half = (position >= heads).astype(jnp.int32)
        return live, half, position - half * heads

    def hide(position):
        live = jnp.logical_or(
            jnp.logical_and(position >= first, position < first + slices),
            jnp.logical_and(position >= second, position < second + slices),
        )
        half = (position >= second).astype(jnp.int32)
        return live, half, position - first - half * (second - first)

    @pl.when(step == 0)
    def _():
        barrier = pltpu.get_barrier_semaphore()
        for axis, size in (("tp", splits), ("seq", n), ("dp", prompts)):
            for offset in range(1, size):
                pl.semaphore_signal(
                    barrier,
                    inc=1,
                    device_id={axis: lax.rem(lax.axis_index(axis) + offset, size)},
                    device_id_type=MESH,
                )

    @pl.when(step < heads)
    def _():
        query, key, value, grad = queries[...], keys[...], values[...], grads[...]
        scores = dot(key, query, 1, 1) * factor
        weights = jnp.exp(scores - jnp.max(scores, axis=0, keepdims=True))
        probability = weights * (1.0 / jnp.sum(weights, axis=0, keepdims=True))
        value_part = dot(probability.astype(LOW), grad, 1, 0).astype(LOW)
        grad_probs = dot(value, grad, 1, 1)
        grad_scores = probability * (
            grad_probs - jnp.sum(probability * grad_probs, axis=0, keepdims=True)
        )
        grad_low = grad_scores.astype(LOW)
        key_part = (dot(grad_low, query, 1, 0) * factor).astype(LOW)
        for kind, side in ((0, key_part), (1, value_part)):
            for half in range(2):
                part[half, step, kind] = rows_of(side, half)
        grad_query[...] = (dot(grad_low, key, 0, 0) * factor).astype(LOW)

    @pl.when(step == 0)
    def _():
        pl.semaphore_wait(pltpu.get_barrier_semaphore(), splits + n + prompts - 3)

    live, half, index = hide(step)

    @pl.when(live)
    def _():
        product = dot(text[half].reshape(half_length, features), out_weight[...], 1, 1)
        product = product.astype(LOW)
        part[half, index, 0] = product[:, :HD]
        part[half, index, 1] = product[:, HD:]

    up_at = step - 2 * me
    down_at = step - 2 * (n - 1 - me)

    live, half, index = attend(up_at)

    @pl.when(jnp.logical_and(live, me == 0))
    def _():
        up_copy(half, index, part).start()
        up_in[half, index] = jnp.zeros(up_in.shape[2:], LOW)

    @pl.when(jnp.logical_and(live, has_low))
    def _():
        up_copy(half, index, up_out).wait_recv()

        @pl.when(has_high)
        def _():
            up_out[half, index] = up_in[half, index] + part[half, index]
            up_copy(half, index, up_out).start()

    live, half, index = attend(down_at)

    @pl.when(jnp.logical_and(live, me == n - 1))
    def _():
        down_copy(half, index, part).start()
        down_in[half, index] = jnp.zeros(down_in.shape[2:], LOW)

    @pl.when(jnp.logical_and(live, has_high))
    def _():
        down_copy(half, index, down_out).wait_recv()

        @pl.when(has_low)
        def _():
            down_out[half, index] = down_in[half, index] + part[half, index]
            down_copy(half, index, down_out).start()

    live, half, index = hide(up_at)
    for place in range(n):

        @pl.when(jnp.logical_and(live, me == place))
        def _():
            if place == 0:
                up_in[half, index, :, :sub] = jnp.zeros((2, sub, HD), LOW)
                if n > 2:
                    high_copy(half, index, part, 2).start()
            elif place == 1:
                if n > 2:
                    high_copy(half, index, up_out, 2).wait_recv()
            else:
                high_copy(half, index, up_out, place).wait_recv()
            if 0 < place < n - 1:
                rest = (place + 1) * sub
                up_out[half, index, :, rest:] = (
                    up_in[half, index, :, rest:] + part[half, index, :, rest:]
                )
                high_copy(half, index, up_out, place + 1).start()

    live, half, index = hide(down_at)
    for place in range(n):

        @pl.when(jnp.logical_and(live, me == place))
        def _():
            if place == n - 1:
                down_in[half, index, :, place * sub :] = jnp.zeros((2, sub, HD), LOW)
                if n > 2:
                    low_copy(half, index, part, n - 3).start()
            elif place == n - 2:
                if n > 2:
                    low_copy(half, index, down_out, n - 3).wait_recv()
            else:
                low_copy(half, index, down_out, place).wait_recv()
            if 0 < place < n - 1:
                rest = place * sub
                down_out[half, index, :, :rest] = (
                    down_in[half, index, :, :rest] + part[half, index, :, :rest]
                )
                low_copy(half, index, down_out, place - 1).start()

    live, half, index = hide(step - plan["delay"])

    @pl.when(jnp.logical_and(live, me == 0))
    def _():
        near_up_copy(half, index).start()

    @pl.when(jnp.logical_and(live, me == n - 1))
    def _():
        near_down_copy(half, index).start()

    @pl.when(step == 0)
    def _():
        total[...] = jnp.zeros_like(total)
        project[...] = jnp.zeros_like(project)
        up_sum[...] = jnp.zeros_like(up_sum)

    def latent_copy(slot, owner, offset):
        return pltpu.make_async_remote_copy(
            src_ref=latent_own.at[owner],
            dst_ref=latent_all.at[slot],
            send_sem=latent_send.at[offset],
            recv_sem=latent_recv.at[slot],
            device_id={"seq": lax.rem(me + offset, n)},
            device_id_type=MESH,
        )

    @pl.when(step == 1)
    def _():
        down = jnp.concatenate([key_down[...], value_down[...]], axis=0)
        sides = [dot(down, context_of(side), 1, 1) for side in range(2)]
        latent_own[...] = (
            jnp.concatenate(sides, axis=1).reshape(latent_own.shape).astype(LOW)
        )
        for offset in range(1, n):
            latent_copy(me, lax.rem(me + offset, n), offset).start()
        latent_all[me] = latent_own[me]

    @pl.when(step == lag - 1)
    def _():
        for offset in range(1, n):
            latent_copy(lax.rem(me + offset, n), me, offset).wait_recv()
        for offset in range(1, n):
            latent_copy(me, lax.rem(me + offset, n), offset).wait_send()
        both = low_sum(latent_all, n).astype(LOW)
        for side in range(2):
            latent[side] = both[:, side * half_length : (side + 1) * half_length]

    live, half, index = attend(step - lag)

    @pl.when(live)
    def _():
        @pl.when(has_high)
        def _():
            up_copy(half, index, up_out).wait_send()

        @pl.when(has_low)
        def _():
            down_copy(half, index, down_out).wait_send()

        both = (
            up_in[half, index].astype(jnp.float32)
            + part[half, index].astype(jnp.float32)
            + down_in[half, index].astype(jnp.float32)
        ).astype(LOW)
        pair = jnp.concatenate([both[0], both[1]], axis=1)
        slab = jnp.concatenate([key_weight[...], value_weight[...]], axis=1)
        total[half] += dot(pair, slab, 1, 1)
        blank = jnp.zeros((rank, HD), LOW)
        rises = jnp.concatenate(
            [
                jnp.concatenate([key_up[...], blank], axis=1),
                jnp.concatenate([blank, value_up[...]], axis=1),
            ],
            axis=0,
        )
        project[half] += dot(pair, rises, 1, 1)
        own = jnp.where(me < n // 2, both[0], both[1])
        up_sum[index] += dot(latent[half], own, 1, 0)

    for side in range(2):
        end = heads * (side + 1) + lag - 1
        project_start, project_finish = exchange(
            "tp", splits, project_all.at[side], project_send.at[side], project_recv.at[side]
        )
        context_start, context_finish = exchange(
            "tp", splits, context_all.at[side], context_send.at[side], context_recv.at[side]
        )
        sum_start, sum_finish = exchange(
            "seq", n, sum_all.at[side], sum_send.at[side], sum_recv.at[side]
        )

        @pl.when(step == end)
        def _():
            project_all[side, split] = project[side].astype(LOW)
            context_all[side, split] = total[side].astype(LOW)
            project_start()
            context_start()

        @pl.when(step == end + 2)
        def _():
            project_finish()
            context_finish()
            back = low_sum(project_all.at[side], splits).astype(LOW)
            low_rank = dot(back[:, :rank], key_down[...], 1, 0) + dot(
                back[:, rank:], value_down[...], 1, 0
            )
            scaled = gain[...] * (low_sum(context_all.at[side], splits) + low_rank)
            total[side] = scaled
            local_sum = jnp.sum(
                rows_of(normed, side).astype(jnp.float32) * scaled, axis=1, keepdims=True
            )
            line = jnp.transpose(jnp.broadcast_to(local_sum, (half_length, 128)))[:1, :]
            sum_all[side, me] = jnp.concatenate(
                [line[:, at : at + 128] for at in range(0, half_length, 128)], axis=0
            )
            sum_start()
            down = dot(back, context_of(side), 0, 0)
            if side == 0:
                down_sum[...] = down
            else:
                down_sum[...] += down

        @pl.when(step == end + 6)
        def _():
            sum_finish()
            token_sum = sum_all[side, 0]
            for other in range(1, n):
                token_sum = token_sum + sum_all[side, other]
            line = jnp.concatenate(
                [token_sum[at : at + 1] for at in range(half_length // 128)], axis=1
            )
            token_column = column(line, half_length)
            result = rows_of(column(scale[...], length), side) * (
                total[side]
                - rows_of(normed, side).astype(jnp.float32)
                * (token_column / plan["features_whole"])
            )
            text[side] = result.astype(LOW).reshape(n, sub, features)
            for owner in range(n):
                pltpu.make_async_copy(
                    text.at[side, owner],
                    grad_text.at[pl.ds(owner * block + side * sub, sub)],
                    text_sem.at[side, owner],
                ).start()

    end = 2 * heads + lag - 1
    portion = up_own.shape[2]

    def up_piece(slot, owner, offset):
        return pltpu.make_async_remote_copy(
            src_ref=up_own.at[owner],
            dst_ref=up_all.at[slot],
            send_sem=up_dp_send.at[offset],
            recv_sem=up_dp_recv.at[slot],
            device_id={"dp": lax.rem(prompt + offset, prompts)},
            device_id_type=MESH,
        )

    whole_start, whole_finish = exchange("dp", prompts, up_whole, whole_send, whole_recv)
    down_start, down_finish = exchange("dp", prompts, down_all, down_dp_send, down_dp_recv)
    rows_start, rows_finish = exchange("seq", n, rows_all, rows_send, rows_recv)

    @pl.when(step == end + 1)
    def _():
        rows = jnp.concatenate([up_sum[index] for index in range(heads)], axis=1).astype(LOW)
        for owner in range(prompts):
            up_own[owner] = rows[:, owner * portion : (owner + 1) * portion]
        for offset in range(1, prompts):
            up_piece(prompt, lax.rem(prompt + offset, prompts), offset).start()
        up_all[prompt] = up_own[prompt]

    @pl.when(step == end + 3)
    def _():
        down_all[prompt] = down_sum[...].astype(LOW)
        down_start()

    @pl.when(step == end + 5)
    def _():
        for offset in range(1, prompts):
            up_piece(lax.rem(prompt + offset, prompts), prompt, offset).wait_recv()
        for offset in range(1, prompts):
            up_piece(prompt, lax.rem(prompt + offset, prompts), offset).wait_send()
        rows_all[me] = (low_sum(up_all, prompts) / prompts).astype(LOW)
        rows_start()

    @pl.when(step == end + 9)
    def _():
        down_finish()
        down = low_sum(down_all, prompts)
        key_down_grad[...] = down[:rank] / prompts
        value_down_grad[...] = down[rank:] / prompts

    @pl.when(step == end + 12)
    def _():
        rows_finish()
        up_whole[prompt] = rows_all[...]
        whole_start()

    @pl.when(step == end + 18)
    def _():
        whole_finish()
        for owner in range(prompts):
            columns = slice(owner * portion, (owner + 1) * portion)
            rows = up_whole[owner].astype(jnp.float32).reshape(2 * rank, portion)
            key_up_grad[:, columns] = rows[:rank]
            value_up_grad[:, columns] = rows[rank:]

    live, half, index = hide(step - lag)
    for place in range(n):

        @pl.when(jnp.logical_and(live, me == place))
        def _():
            if place == 0:
                near_up_copy(half, index).wait_send()
            if place == 1:
                near_up_copy(half, index).wait_recv()
            if place == n - 2:
                near_down_copy(half, index).wait_recv()
            if place == n - 1:
                near_down_copy(half, index).wait_send()
            if place < n - 1 and n > 2:
                high_copy(half, index, up_out, max(place + 1, 2)).wait_send()
            if place > 0 and n > 2:
                low_copy(half, index, down_out, min(place - 1, n - 3)).wait_send()
            own = slice(place * sub, (place + 1) * sub)
            both = (
                up_in[half, index, :, own].astype(jnp.float32)
                + part[half, index, :, own].astype(jnp.float32)
                + down_in[half, index, :, own].astype(jnp.float32)
            ).astype(LOW)
            grad_hidden[...] = jnp.concatenate([both[0], both[1]], axis=1)

    @pl.when(step == steps - 1)
    def _():
        for side in range(2):
            for owner in range(n):
                pltpu.make_async_copy(
                    text.at[side, owner],
                    grad_text.at[pl.ds(owner * block + side * sub, sub)],
                    text_sem.at[side, owner],
                ).wait()


def store_kernel(count, pieces, *refs):
    sources, results, stages = refs[:count], refs[count : 2 * count], refs[2 * count : 3 * count]
    load_sem, store_sem = refs[3 * count :]

    def copies(item, piece):
        rows = sources[item].shape[0] // pieces[item]
        at = pl.ds(piece * rows, rows)
        slot = sum(pieces[:item]) + piece
        return (
            pltpu.make_async_copy(
                sources[item].at[at], stages[item].at[at], load_sem.at[slot]
            ),
            pltpu.make_async_copy(
                stages[item].at[at], results[item].at[at], store_sem.at[slot]
            ),
        )

    every = [copies(item, piece) for item in range(count) for piece in range(pieces[item])]
    for load, _ in every:
        load.start()
    for load, store in every:
        load.wait()
        store.start()
    for _, store in every:
        store.wait()


def store(*arrays):
    pieces = [
        2 if value.shape[0] % 64 == 0 and value.size >= 2**18 else 1 for value in arrays
    ]
    total = sum(pieces)
    anywhere = pl.BlockSpec(memory_space=pl.ANY)
    return pl.pallas_call(
        functools.partial(store_kernel, len(arrays), pieces),
        out_shape=tuple(jax.ShapeDtypeStruct(value.shape, value.dtype) for value in arrays),
        in_specs=[anywhere] * len(arrays),
        out_specs=(anywhere,) * len(arrays),
        scratch_shapes=[pltpu.VMEM(value.shape, value.dtype) for value in arrays]
        + [pltpu.SemaphoreType.DMA((total,))] * 2,
        name="store",
    )(*arrays)


def shards(
    queries,
    keys,
    values,
    grad_attention,
    normed,
    norm_scale,
    norm_gain,
    key_weight,
    value_weight,
    key_down,
    key_up,
    value_down,
    value_up,
    out_weight,
):
    rows, columns = queries.shape[1:]
    length, features = normed.shape[1:]
    rank = key_up.shape[0]
    hidden = out_weight.shape[0]
    n, splits, prompts = lax.axis_size("seq"), lax.axis_size("tp"), lax.axis_size("dp")
    heads = columns // HD
    width = 2 * HD
    slices = hidden // width
    lag = 2 * (n - 1)
    first = max(2 * heads, heads + lag + 6)
    second = max(first + slices, 2 * heads + lag + 6)
    steps = max(second + slices + lag, 2 * heads + lag + 18)
    block = length // n
    sub = block // 2
    half_length = length // 2
    share = 2 * rank // n
    plan = dict(
        n=n,
        splits=splits,
        prompts=prompts,
        heads=heads,
        slices=slices,
        lag=lag,
        ring=lag + 4,
        delay=max(0, min(4, lag - 2)),
        first=first,
        second=second,
        steps=steps,
        features_whole=features * n,
    )

    def early(height):
        return pl.BlockSpec((height, HD), lambda step: (0, jnp.minimum(step, heads - 1)))

    def late(height):
        def place(step):
            at = jnp.clip(step - lag, 0, 2 * heads - 1)
            return 0, at - jnp.where(at >= heads, heads, 0)

        return pl.BlockSpec((height, HD), place)

    def fixed(height, size):
        return pl.BlockSpec((height, size), lambda step: (0, 0))

    def slice_of(step):
        after = step >= second
        return after.astype(jnp.int32), jnp.clip(
            step - jnp.where(after, second, first), 0, slices - 1
        )

    buffer = pltpu.VMEM((2, max(heads, slices), 2, half_length, HD), LOW)
    dma = pltpu.SemaphoreType.DMA
    grad_query, grad_hidden, grad_text, down_key, down_value, up_key, up_value = pl.pallas_call(
        functools.partial(kernel, plan),
        grid=(steps,),
        out_shape=(
            jax.ShapeDtypeStruct((rows, columns), LOW),
            jax.ShapeDtypeStruct((block, hidden), LOW),
            jax.ShapeDtypeStruct((length, features), LOW),
            jax.ShapeDtypeStruct((rank, features), jnp.float32),
            jax.ShapeDtypeStruct((rank, features), jnp.float32),
            jax.ShapeDtypeStruct((rank, columns), jnp.float32),
            jax.ShapeDtypeStruct((rank, columns), jnp.float32),
        ),
        in_specs=[
            early(rows),
            early(length),
            early(length),
            early(rows),
            late(features),
            late(features),
            late(rank),
            late(rank),
            pl.BlockSpec((width, features), lambda step: (slice_of(step)[1], 0)),
            fixed(length, features),
            fixed(1, length),
            fixed(1, features),
            fixed(rank, features),
            fixed(rank, features),
        ],
        out_specs=(
            early(rows),
            pl.BlockSpec((sub, width), lambda step: slice_of(step - lag)),
            pl.BlockSpec(memory_space=pl.ANY),
            fixed(rank, features),
            fixed(rank, features),
            fixed(rank, columns),
            fixed(rank, columns),
        ),
        scratch_shapes=[buffer] * 5
        + [
            pltpu.VMEM((2, half_length, features), jnp.float32),
            pltpu.VMEM((2, half_length, 2 * rank), jnp.float32),
            pltpu.VMEM((2, splits, half_length, features), LOW),
            pltpu.VMEM((2, splits, half_length, 2 * rank), LOW),
            pltpu.VMEM((2, n, sub, features), LOW),
            pltpu.VMEM((2, n, half_length // 128, 128), jnp.float32),
            pltpu.VMEM((n, share, length), LOW),
            pltpu.VMEM((n, share, length), LOW),
            pltpu.VMEM((2, share, half_length), LOW),
            pltpu.VMEM((heads, share, HD), jnp.float32),
            pltpu.VMEM((prompts, share, columns // prompts), LOW),
            pltpu.VMEM((prompts, share, columns // prompts), LOW),
            pltpu.VMEM((n, share, columns // prompts), LOW),
            pltpu.VMEM((prompts, n, share, columns // prompts), LOW),
            pltpu.VMEM((2 * rank, features), jnp.float32),
            pltpu.VMEM((prompts, 2 * rank, features), LOW),
        ]
        + [dma((lag + 4,))] * 4
        + [dma((2, splits))] * 4
        + [dma((2, n))] * 2
        + [dma((n,))] * 2
        + [dma((prompts,))] * 4
        + [dma((n,))] * 2
        + [dma((prompts,))] * 2
        + [dma((lag + 4,))] * 4
        + [dma((2, n))],
        compiler_params=pltpu.CompilerParams(
            collective_id=0, has_side_effects=True, vmem_limit_bytes=62 * 1024 * 1024
        ),
        name="fused",
    )(
        queries[0],
        keys[0],
        values[0],
        grad_attention[0],
        key_weight,
        value_weight,
        key_up,
        value_up,
        out_weight,
        normed[0],
        norm_scale,
        norm_gain[None, :],
        key_down.T,
        value_down.T,
    )
    grad_query, grad_hidden, grad_text, down_key, down_value, up_key, up_value = store(
        grad_query, grad_hidden, grad_text, down_key, down_value, up_key, up_value
    )
    return (
        grad_query[None],
        grad_text[None],
        grad_hidden[None],
        down_key.T,
        up_key,
        down_value.T,
        up_value,
    )


def solution(mesh):
    return jax.shard_map(
        shards,
        mesh=mesh,
        in_specs=(
            P("dp", "seq", "tp"),
            P("dp", None, "tp"),
            P("dp", None, "tp"),
            P("dp", "seq", "tp"),
            P("dp", None, "seq"),
            P("dp", None),
            P("seq"),
            P("seq", "tp"),
            P("seq", "tp"),
            P("seq", None),
            P(None, "tp"),
            P("seq", None),
            P(None, "tp"),
            P("tp", "seq"),
        ),
        out_specs=(
            P("dp", "seq", "tp"),
            P("dp", None, "seq"),
            P("dp", "seq", "tp"),
            P("seq", None),
            P(None, "tp"),
            P("seq", None),
            P(None, "tp"),
        ),
        check_vma=False,
    )
```

```python
import functools

import jax
import jax.numpy as jnp
from jax import lax
from jax.experimental import pallas as pl
from jax.experimental.pallas import tpu as pltpu
from jax.sharding import PartitionSpec as P

HD = 128
MESH = pl.DeviceIdType.MESH
LOW = jnp.bfloat16


def dot(left_side, right_side, left_dim, right_dim):
    return lax.dot_general(
        left_side,
        right_side,
        (((left_dim,), (right_dim,)), ((), ())),
        preferred_element_type=jnp.float32,
    )


def exchange(axis, size, landing, send, recv):
    me = lax.axis_index(axis)

    def copy(slot, offset):
        return pltpu.make_async_remote_copy(
            src_ref=landing.at[slot],
            dst_ref=landing.at[slot],
            send_sem=send.at[offset],
            recv_sem=recv.at[slot],
            device_id={axis: lax.rem(me + offset, size)},
            device_id_type=MESH,
        )

    def start():
        for offset in range(1, size):
            copy(me, offset).start()

    def finish():
        for offset in range(1, size):
            copy(lax.rem(me + offset, size), offset).wait_recv()
        for offset in range(1, size):
            copy(me, offset).wait_send()

    return start, finish


def low_sum(ref, size):
    value = ref[0].astype(jnp.float32)
    for index in range(1, size):
        value = value + ref[index].astype(jnp.float32)
    return value


def kernel(
    plan,
    queries,
    keys,
    values,
    grads,
    key_weight,
    value_weight,
    key_up,
    value_up,
    out_weight,
    normed,
    scale,
    gain,
    key_down,
    value_down,
    grad_query,
    grad_hidden,
    grad_text,
    key_down_grad,
    value_down_grad,
    key_up_grad,
    value_up_grad,
    part,
    up_in,
    up_out,
    down_in,
    down_out,
    total,
    project,
    context_all,
    project_all,
    text,
    sum_all,
    latent_own,
    latent_all,
    latent,
    up_sum,
    up_own,
    up_all,
    rows_all,
    up_whole,
    down_sum,
    down_all,
    up_send,
    up_recv,
    down_send,
    down_recv,
    context_send,
    context_recv,
    project_send,
    project_recv,
    sum_send,
    sum_recv,
    latent_send,
    latent_recv,
    up_dp_send,
    up_dp_recv,
    down_dp_send,
    down_dp_recv,
    rows_send,
    rows_recv,
    whole_send,
    whole_recv,
    near_up_send,
    near_up_recv,
    near_down_send,
    near_down_recv,
    text_sem,
):
    n, splits, prompts = plan["n"], plan["splits"], plan["prompts"]
    heads, slices, lag = plan["heads"], plan["slices"], plan["lag"]
    first, second, steps = plan["first"], plan["second"], plan["steps"]
    length, features = normed.shape
    block = length // n
    sub = block // 2
    half_length = length // 2
    rank = key_down.shape[0]
    step = pl.program_id(0)
    me = lax.axis_index("seq")
    split = lax.axis_index("tp")
    prompt = lax.axis_index("dp")
    factor = HD ** (-0.5)
    above = lax.rem(me + 1, n)
    below = lax.rem(me + n - 1, n)
    has_low = me > 0
    has_high = me < n - 1

    def rows_of(value, half):
        return jnp.concatenate(
            [
                value[owner * block + half * sub : owner * block + half * sub + sub]
                for owner in range(n)
            ],
            axis=0,
        )

    def context_of(half):
        return (rows_of(normed, half).astype(jnp.float32) * gain[...]).astype(LOW)

    def column(row, size):
        return jnp.transpose(jnp.broadcast_to(row, (128, size)))[:, :1]

    ring = plan["ring"]

    def heads_ring(half, index):
        return lax.rem(index + half * heads, ring)

    def hidden_ring(half, index):
        return lax.rem(first + index + half * (second - first), ring)

    def up_copy(half, index, source):
        return pltpu.make_async_remote_copy(
            src_ref=source.at[half, index],
            dst_ref=up_in.at[half, index],
            send_sem=up_send.at[heads_ring(half, index)],
            recv_sem=up_recv.at[heads_ring(half, index)],
            device_id={"seq": above},
            device_id_type=MESH,
        )

    def down_copy(half, index, source):
        return pltpu.make_async_remote_copy(
            src_ref=source.at[half, index],
            dst_ref=down_in.at[half, index],
            send_sem=down_send.at[heads_ring(half, index)],
            recv_sem=down_recv.at[heads_ring(half, index)],
            device_id={"seq": below},
            device_id_type=MESH,
        )

    def high_copy(half, index, source, owner):
        rows = pl.ds(owner * sub, (n - owner) * sub)
        return pltpu.make_async_remote_copy(
            src_ref=source.at[half, index, :, rows],
            dst_ref=up_in.at[half, index, :, rows],
            send_sem=up_send.at[hidden_ring(half, index)],
            recv_sem=up_recv.at[hidden_ring(half, index)],
            device_id={"seq": above},
            device_id_type=MESH,
        )

    def low_copy(half, index, source, owner):
        rows = pl.ds(0, (owner + 1) * sub)
        return pltpu.make_async_remote_copy(
            src_ref=source.at[half, index, :, rows],
            dst_ref=down_in.at[half, index, :, rows],
            send_sem=down_send.at[hidden_ring(half, index)],
            recv_sem=down_recv.at[hidden_ring(half, index)],
            device_id={"seq": below},
            device_id_type=MESH,
        )

    def near_up_copy(half, index):
        rows = pl.ds(sub, sub)
        return pltpu.make_async_remote_copy(
            src_ref=part.at[half, index, :, rows],
            dst_ref=up_in.at[half, index, :, rows],
            send_sem=near_up_send.at[hidden_ring(half, index)],
            recv_sem=near_up_recv.at[hidden_ring(half, index)],
            device_id={"seq": above},
            device_id_type=MESH,
        )

    def near_down_copy(half, index):
        rows = pl.ds((n - 2) * sub, sub)
        return pltpu.make_async_remote_copy(
            src_ref=part.at[half, index, :, rows],
            dst_ref=down_in.at[half, index, :, rows],
            send_sem=near_down_send.at[hidden_ring(half, index)],
            recv_sem=near_down_recv.at[hidden_ring(half, index)],
            device_id={"seq": below},
            device_id_type=MESH,
        )

    def attend(position):
        live = jnp.logical_and(position >= 0, position < 2 * heads)
        half = (position >= heads).astype(jnp.int32)
        return live, half, position - half * heads

    def hide(position):
        live = jnp.logical_or(
            jnp.logical_and(position >= first, position < first + slices),
            jnp.logical_and(position >= second, position < second + slices),
        )
        half = (position >= second).astype(jnp.int32)
        return live, half, position - first - half * (second - first)

    @pl.when(step == 0)
    def _():
        barrier = pltpu.get_barrier_semaphore()
        for axis, size in (("tp", splits), ("seq", n), ("dp", prompts)):
            for offset in range(1, size):
                pl.semaphore_signal(
                    barrier,
                    inc=1,
                    device_id={axis: lax.rem(lax.axis_index(axis) + offset, size)},
                    device_id_type=MESH,
                )

    @pl.when(step < heads)
    def _():
        query, key, value, grad = queries[...], keys[...], values[...], grads[...]
        scores = dot(key, query, 1, 1) * factor
        weights = jnp.exp(scores - jnp.max(scores, axis=0, keepdims=True))
        probability = weights * (1.0 / jnp.sum(weights, axis=0, keepdims=True))
        value_part = dot(probability.astype(LOW), grad, 1, 0).astype(LOW)
        grad_probs = dot(value, grad, 1, 1)
        grad_scores = probability * (
            grad_probs - jnp.sum(probability * grad_probs, axis=0, keepdims=True)
        )
        grad_low = grad_scores.astype(LOW)
        key_part = (dot(grad_low, query, 1, 0) * factor).astype(LOW)
        for kind, side in ((0, key_part), (1, value_part)):
            for half in range(2):
                part[half, step, kind] = rows_of(side, half)
        grad_query[...] = (dot(grad_low, key, 0, 0) * factor).astype(LOW)

    @pl.when(step == 0)
    def _():
        pl.semaphore_wait(pltpu.get_barrier_semaphore(), splits + n + prompts - 3)

    live, half, index = hide(step)

    @pl.when(live)
    def _():
        product = dot(text[half].reshape(half_length, features), out_weight[...], 1, 1)
        product = product.astype(LOW)
        part[half, index, 0] = product[:, :HD]
        part[half, index, 1] = product[:, HD:]

    up_at = step - plan["spacing"] * me
    down_at = step - plan["spacing"] * (n - 1 - me)

    live, half, index = attend(up_at)

    @pl.when(jnp.logical_and(live, me == 0))
    def _():
        up_copy(half, index, part).start()
        up_in[half, index] = jnp.zeros(up_in.shape[2:], LOW)

    @pl.when(jnp.logical_and(live, has_low))
    def _():
        up_copy(half, index, up_out).wait_recv()

        @pl.when(has_high)
        def _():
            up_out[half, index] = up_in[half, index] + part[half, index]
            up_copy(half, index, up_out).start()

    live, half, index = attend(down_at)

    @pl.when(jnp.logical_and(live, me == n - 1))
    def _():
        down_copy(half, index, part).start()
        down_in[half, index] = jnp.zeros(down_in.shape[2:], LOW)

    @pl.when(jnp.logical_and(live, has_high))
    def _():
        down_copy(half, index, down_out).wait_recv()

        @pl.when(has_low)
        def _():
            down_out[half, index] = down_in[half, index] + part[half, index]
            down_copy(half, index, down_out).start()

    live, half, index = hide(up_at)
    for place in range(n):

        @pl.when(jnp.logical_and(live, me == place))
        def _():
            if place == 0:
                up_in[half, index, :, :sub] = jnp.zeros((2, sub, HD), LOW)
                if n > 2:
                    high_copy(half, index, part, 2).start()
            elif place == 1:
                if n > 2:
                    high_copy(half, index, up_out, 2).wait_recv()
            else:
                high_copy(half, index, up_out, place).wait_recv()
            if 0 < place < n - 1:
                rest = (place + 1) * sub
                up_out[half, index, :, rest:] = (
                    up_in[half, index, :, rest:] + part[half, index, :, rest:]
                )
                high_copy(half, index, up_out, place + 1).start()

    live, half, index = hide(down_at)
    for place in range(n):

        @pl.when(jnp.logical_and(live, me == place))
        def _():
            if place == n - 1:
                down_in[half, index, :, place * sub :] = jnp.zeros((2, sub, HD), LOW)
                if n > 2:
                    low_copy(half, index, part, n - 3).start()
            elif place == n - 2:
                if n > 2:
                    low_copy(half, index, down_out, n - 3).wait_recv()
            else:
                low_copy(half, index, down_out, place).wait_recv()
            if 0 < place < n - 1:
                rest = place * sub
                down_out[half, index, :, :rest] = (
                    down_in[half, index, :, :rest] + part[half, index, :, :rest]
                )
                low_copy(half, index, down_out, place - 1).start()

    live, half, index = hide(step - plan["delay"])

    @pl.when(jnp.logical_and(live, me == 0))
    def _():
        near_up_copy(half, index).start()

    @pl.when(jnp.logical_and(live, me == n - 1))
    def _():
        near_down_copy(half, index).start()

    @pl.when(step == 0)
    def _():
        total[...] = jnp.zeros_like(total)
        project[...] = jnp.zeros_like(project)
        up_sum[...] = jnp.zeros_like(up_sum)

    def latent_copy(slot, owner, offset):
        return pltpu.make_async_remote_copy(
            src_ref=latent_own.at[owner],
            dst_ref=latent_all.at[slot],
            send_sem=latent_send.at[offset],
            recv_sem=latent_recv.at[slot],
            device_id={"seq": lax.rem(me + offset, n)},
            device_id_type=MESH,
        )

    @pl.when(step == 1)
    def _():
        down = jnp.concatenate([key_down[...], value_down[...]], axis=0)
        sides = [dot(down, context_of(side), 1, 1) for side in range(2)]
        latent_own[...] = (
            jnp.concatenate(sides, axis=1).reshape(latent_own.shape).astype(LOW)
        )
        for offset in range(1, n):
            latent_copy(me, lax.rem(me + offset, n), offset).start()
        latent_all[me] = latent_own[me]

    @pl.when(step == lag - 1)
    def _():
        for offset in range(1, n):
            latent_copy(lax.rem(me + offset, n), me, offset).wait_recv()
        for offset in range(1, n):
            latent_copy(me, lax.rem(me + offset, n), offset).wait_send()
        both = low_sum(latent_all, n).astype(LOW)
        for side in range(2):
            latent[side] = both[:, side * half_length : (side + 1) * half_length]

    live, half, index = attend(step - lag)

    @pl.when(live)
    def _():
        @pl.when(has_high)
        def _():
            up_copy(half, index, up_out).wait_send()

        @pl.when(has_low)
        def _():
            down_copy(half, index, down_out).wait_send()

        both = (
            up_in[half, index].astype(jnp.float32)
            + part[half, index].astype(jnp.float32)
            + down_in[half, index].astype(jnp.float32)
        ).astype(LOW)
        pair = jnp.concatenate([both[0], both[1]], axis=1)
        slab = jnp.concatenate([key_weight[...], value_weight[...]], axis=1)
        total[half] += dot(pair, slab, 1, 1)
        blank = jnp.zeros((rank, HD), LOW)
        rises = jnp.concatenate(
            [
                jnp.concatenate([key_up[...], blank], axis=1),
                jnp.concatenate([blank, value_up[...]], axis=1),
            ],
            axis=0,
        )
        project[half] += dot(pair, rises, 1, 1)
        own = jnp.where(me < n // 2, both[0], both[1])
        up_sum[index] += dot(latent[half], own, 1, 0)

    for side in range(2):
        end = heads * (side + 1) + lag - 1
        project_start, project_finish = exchange(
            "tp", splits, project_all.at[side], project_send.at[side], project_recv.at[side]
        )
        context_start, context_finish = exchange(
            "tp", splits, context_all.at[side], context_send.at[side], context_recv.at[side]
        )
        sum_start, sum_finish = exchange(
            "seq", n, sum_all.at[side], sum_send.at[side], sum_recv.at[side]
        )

        @pl.when(step == end)
        def _():
            project_all[side, split] = project[side].astype(LOW)
            context_all[side, split] = total[side].astype(LOW)
            project_start()
            context_start()

        @pl.when(step == end + 2)
        def _():
            project_finish()
            context_finish()
            back = low_sum(project_all.at[side], splits).astype(LOW)
            low_rank = dot(back[:, :rank], key_down[...], 1, 0) + dot(
                back[:, rank:], value_down[...], 1, 0
            )
            scaled = gain[...] * (low_sum(context_all.at[side], splits) + low_rank)
            total[side] = scaled
            local_sum = jnp.sum(
                rows_of(normed, side).astype(jnp.float32) * scaled, axis=1, keepdims=True
            )
            line = jnp.transpose(jnp.broadcast_to(local_sum, (half_length, 128)))[:1, :]
            sum_all[side, me] = jnp.concatenate(
                [line[:, at : at + 128] for at in range(0, half_length, 128)], axis=0
            )
            sum_start()
            down = dot(back, context_of(side), 0, 0)
            if side == 0:
                down_sum[...] = down
            else:
                down_sum[...] += down

        @pl.when(step == end + 6)
        def _():
            sum_finish()
            token_sum = sum_all[side, 0]
            for other in range(1, n):
                token_sum = token_sum + sum_all[side, other]
            line = jnp.concatenate(
                [token_sum[at : at + 1] for at in range(half_length // 128)], axis=1
            )
            token_column = column(line, half_length)
            result = rows_of(column(scale[...], length), side) * (
                total[side]
                - rows_of(normed, side).astype(jnp.float32)
                * (token_column / plan["features_whole"])
            )
            text[side] = result.astype(LOW).reshape(n, sub, features)
            for owner in range(n):
                pltpu.make_async_copy(
                    text.at[side, owner],
                    grad_text.at[pl.ds(owner * block + side * sub, sub)],
                    text_sem.at[side, owner],
                ).start()

    end = 2 * heads + lag - 1
    portion = up_own.shape[2]

    def up_piece(slot, owner, offset):
        return pltpu.make_async_remote_copy(
            src_ref=up_own.at[owner],
            dst_ref=up_all.at[slot],
            send_sem=up_dp_send.at[offset],
            recv_sem=up_dp_recv.at[slot],
            device_id={"dp": lax.rem(prompt + offset, prompts)},
            device_id_type=MESH,
        )

    whole_start, whole_finish = exchange("dp", prompts, up_whole, whole_send, whole_recv)
    down_start, down_finish = exchange("dp", prompts, down_all, down_dp_send, down_dp_recv)
    rows_start, rows_finish = exchange("seq", n, rows_all, rows_send, rows_recv)

    @pl.when(step == end + 1)
    def _():
        rows = jnp.concatenate([up_sum[index] for index in range(heads)], axis=1).astype(LOW)
        for owner in range(prompts):
            up_own[owner] = rows[:, owner * portion : (owner + 1) * portion]
        for offset in range(1, prompts):
            up_piece(prompt, lax.rem(prompt + offset, prompts), offset).start()
        up_all[prompt] = up_own[prompt]

    @pl.when(step == end + 3)
    def _():
        down_all[prompt] = down_sum[...].astype(LOW)
        down_start()

    @pl.when(step == end + 5)
    def _():
        for offset in range(1, prompts):
            up_piece(lax.rem(prompt + offset, prompts), prompt, offset).wait_recv()
        for offset in range(1, prompts):
            up_piece(prompt, lax.rem(prompt + offset, prompts), offset).wait_send()
        rows_all[me] = (low_sum(up_all, prompts) / prompts).astype(LOW)
        rows_start()

    @pl.when(step == end + 9)
    def _():
        down_finish()
        down = low_sum(down_all, prompts)
        key_down_grad[...] = down[:rank] / prompts
        value_down_grad[...] = down[rank:] / prompts

    @pl.when(step == end + 12)
    def _():
        rows_finish()
        up_whole[prompt] = rows_all[...]
        whole_start()

    @pl.when(step == end + 18)
    def _():
        whole_finish()
        for owner in range(prompts):
            columns = slice(owner * portion, (owner + 1) * portion)
            rows = up_whole[owner].astype(jnp.float32).reshape(2 * rank, portion)
            key_up_grad[:, columns] = rows[:rank]
            value_up_grad[:, columns] = rows[rank:]

    live, half, index = hide(step - lag)
    for place in range(n):

        @pl.when(jnp.logical_and(live, me == place))
        def _():
            if place == 0:
                near_up_copy(half, index).wait_send()
            if place == 1:
                near_up_copy(half, index).wait_recv()
            if place == n - 2:
                near_down_copy(half, index).wait_recv()
            if place == n - 1:
                near_down_copy(half, index).wait_send()
            if place < n - 1 and n > 2:
                high_copy(half, index, up_out, max(place + 1, 2)).wait_send()
            if place > 0 and n > 2:
                low_copy(half, index, down_out, min(place - 1, n - 3)).wait_send()
            own = slice(place * sub, (place + 1) * sub)
            both = (
                up_in[half, index, :, own].astype(jnp.float32)
                + part[half, index, :, own].astype(jnp.float32)
                + down_in[half, index, :, own].astype(jnp.float32)
            ).astype(LOW)
            grad_hidden[...] = jnp.concatenate([both[0], both[1]], axis=1)

    @pl.when(step == steps - 1)
    def _():
        for side in range(2):
            for owner in range(n):
                pltpu.make_async_copy(
                    text.at[side, owner],
                    grad_text.at[pl.ds(owner * block + side * sub, sub)],
                    text_sem.at[side, owner],
                ).wait()


def store_kernel(count, pieces, *refs):
    sources, results, stages = refs[:count], refs[count : 2 * count], refs[2 * count : 3 * count]
    load_sem, store_sem = refs[3 * count :]

    def copies(item, piece):
        rows = sources[item].shape[0] // pieces[item]
        at = pl.ds(piece * rows, rows)
        slot = sum(pieces[:item]) + piece
        return (
            pltpu.make_async_copy(
                sources[item].at[at], stages[item].at[at], load_sem.at[slot]
            ),
            pltpu.make_async_copy(
                stages[item].at[at], results[item].at[at], store_sem.at[slot]
            ),
        )

    every = [copies(item, piece) for item in range(count) for piece in range(pieces[item])]
    for load, _ in every:
        load.start()
    for load, store in every:
        load.wait()
        store.start()
    for _, store in every:
        store.wait()


def store(*arrays):
    pieces = [
        2 if value.shape[0] % 64 == 0 and value.size >= 2**18 else 1 for value in arrays
    ]
    total = sum(pieces)
    anywhere = pl.BlockSpec(memory_space=pl.ANY)
    return pl.pallas_call(
        functools.partial(store_kernel, len(arrays), pieces),
        out_shape=tuple(jax.ShapeDtypeStruct(value.shape, value.dtype) for value in arrays),
        in_specs=[anywhere] * len(arrays),
        out_specs=(anywhere,) * len(arrays),
        scratch_shapes=[pltpu.VMEM(value.shape, value.dtype) for value in arrays]
        + [pltpu.SemaphoreType.DMA((total,))] * 2,
        name="store",
    )(*arrays)


def shards(
    queries,
    keys,
    values,
    grad_attention,
    normed,
    norm_scale,
    norm_gain,
    key_weight,
    value_weight,
    key_down,
    key_up,
    value_down,
    value_up,
    out_weight,
):
    rows, columns = queries.shape[1:]
    length, features = normed.shape[1:]
    rank = key_up.shape[0]
    hidden = out_weight.shape[0]
    n, splits, prompts = lax.axis_size("seq"), lax.axis_size("tp"), lax.axis_size("dp")
    heads = columns // HD
    width = 2 * HD
    slices = hidden // width
    spacing = 3
    lag = spacing * (n - 1)
    first = max(2 * heads, heads + lag + 6)
    second = max(first + slices, 2 * heads + lag + 6)
    steps = max(second + slices + lag, 2 * heads + lag + 18)
    ring = lag + spacing + 2
    block = length // n
    sub = block // 2
    half_length = length // 2
    share = 2 * rank // n
    plan = dict(
        n=n,
        splits=splits,
        prompts=prompts,
        heads=heads,
        slices=slices,
        lag=lag,
        spacing=spacing,
        ring=ring,
        delay=max(0, min(4, lag - 2)),
        first=first,
        second=second,
        steps=steps,
        features_whole=features * n,
    )

    def early(height):
        return pl.BlockSpec((height, HD), lambda step: (0, jnp.minimum(step, heads - 1)))

    def late(height):
        def place(step):
            at = jnp.clip(step - lag, 0, 2 * heads - 1)
            return 0, at - jnp.where(at >= heads, heads, 0)

        return pl.BlockSpec((height, HD), place)

    def fixed(height, size):
        return pl.BlockSpec((height, size), lambda step: (0, 0))

    def slice_of(step):
        after = step >= second
        return after.astype(jnp.int32), jnp.clip(
            step - jnp.where(after, second, first), 0, slices - 1
        )

    buffer = pltpu.VMEM((2, max(heads, slices), 2, half_length, HD), LOW)
    dma = pltpu.SemaphoreType.DMA
    grad_query, grad_hidden, grad_text, down_key, down_value, up_key, up_value = pl.pallas_call(
        functools.partial(kernel, plan),
        grid=(steps,),
        out_shape=(
            jax.ShapeDtypeStruct((rows, columns), LOW),
            jax.ShapeDtypeStruct((block, hidden), LOW),
            jax.ShapeDtypeStruct((length, features), LOW),
            jax.ShapeDtypeStruct((rank, features), jnp.float32),
            jax.ShapeDtypeStruct((rank, features), jnp.float32),
            jax.ShapeDtypeStruct((rank, columns), jnp.float32),
            jax.ShapeDtypeStruct((rank, columns), jnp.float32),
        ),
        in_specs=[
            early(rows),
            early(length),
            early(length),
            early(rows),
            late(features),
            late(features),
            late(rank),
            late(rank),
            pl.BlockSpec((width, features), lambda step: (slice_of(step)[1], 0)),
            fixed(length, features),
            fixed(1, length),
            fixed(1, features),
            fixed(rank, features),
            fixed(rank, features),
        ],
        out_specs=(
            early(rows),
            pl.BlockSpec((sub, width), lambda step: slice_of(step - lag)),
            pl.BlockSpec(memory_space=pl.ANY),
            fixed(rank, features),
            fixed(rank, features),
            fixed(rank, columns),
            fixed(rank, columns),
        ),
        scratch_shapes=[buffer] * 5
        + [
            pltpu.VMEM((2, half_length, features), jnp.float32),
            pltpu.VMEM((2, half_length, 2 * rank), jnp.float32),
            pltpu.VMEM((2, splits, half_length, features), LOW),
            pltpu.VMEM((2, splits, half_length, 2 * rank), LOW),
            pltpu.VMEM((2, n, sub, features), LOW),
            pltpu.VMEM((2, n, half_length // 128, 128), jnp.float32),
            pltpu.VMEM((n, share, length), LOW),
            pltpu.VMEM((n, share, length), LOW),
            pltpu.VMEM((2, share, half_length), LOW),
            pltpu.VMEM((heads, share, HD), jnp.float32),
            pltpu.VMEM((prompts, share, columns // prompts), LOW),
            pltpu.VMEM((prompts, share, columns // prompts), LOW),
            pltpu.VMEM((n, share, columns // prompts), LOW),
            pltpu.VMEM((prompts, n, share, columns // prompts), LOW),
            pltpu.VMEM((2 * rank, features), jnp.float32),
            pltpu.VMEM((prompts, 2 * rank, features), LOW),
        ]
        + [dma((ring,))] * 4
        + [dma((2, splits))] * 4
        + [dma((2, n))] * 2
        + [dma((n,))] * 2
        + [dma((prompts,))] * 4
        + [dma((n,))] * 2
        + [dma((prompts,))] * 2
        + [dma((ring,))] * 4
        + [dma((2, n))],
        compiler_params=pltpu.CompilerParams(
            collective_id=0, has_side_effects=True, vmem_limit_bytes=62 * 1024 * 1024
        ),
        name="fused",
    )(
        queries[0],
        keys[0],
        values[0],
        grad_attention[0],
        key_weight,
        value_weight,
        key_up,
        value_up,
        out_weight,
        normed[0],
        norm_scale,
        norm_gain[None, :],
        key_down.T,
        value_down.T,
    )
    grad_query, grad_hidden, grad_text, down_key, down_value, up_key, up_value = store(
        grad_query, grad_hidden, grad_text, down_key, down_value, up_key, up_value
    )
    return (
        grad_query[None],
        grad_text[None],
        grad_hidden[None],
        down_key.T,
        up_key,
        down_value.T,
        up_value,
    )


def solution(mesh):
    return jax.shard_map(
        shards,
        mesh=mesh,
        in_specs=(
            P("dp", "seq", "tp"),
            P("dp", None, "tp"),
            P("dp", None, "tp"),
            P("dp", "seq", "tp"),
            P("dp", None, "seq"),
            P("dp", None),
            P("seq"),
            P("seq", "tp"),
            P("seq", "tp"),
            P("seq", None),
            P(None, "tp"),
            P("seq", None),
            P(None, "tp"),
            P("tp", "seq"),
        ),
        out_specs=(
            P("dp", "seq", "tp"),
            P("dp", None, "seq"),
            P("dp", "seq", "tp"),
            P("seq", None),
            P(None, "tp"),
            P("seq", None),
            P(None, "tp"),
        ),
        check_vma=False,
    )
```

```python
import functools

import jax
import jax.numpy as jnp
from jax import lax
from jax.experimental import pallas as pl
from jax.experimental.pallas import tpu as pltpu
from jax.sharding import PartitionSpec as P

HD = 128
MESH = pl.DeviceIdType.MESH
LOW = jnp.bfloat16


def dot(left_side, right_side, left_dim, right_dim):
    return lax.dot_general(
        left_side,
        right_side,
        (((left_dim,), (right_dim,)), ((), ())),
        preferred_element_type=jnp.float32,
    )


def exchange(axis, size, landing, send, recv):
    me = lax.axis_index(axis)

    def copy(slot, offset):
        return pltpu.make_async_remote_copy(
            src_ref=landing.at[slot],
            dst_ref=landing.at[slot],
            send_sem=send.at[offset],
            recv_sem=recv.at[slot],
            device_id={axis: lax.rem(me + offset, size)},
            device_id_type=MESH,
        )

    def start():
        for offset in range(1, size):
            copy(me, offset).start()

    def finish():
        for offset in range(1, size):
            copy(lax.rem(me + offset, size), offset).wait_recv()
        for offset in range(1, size):
            copy(me, offset).wait_send()

    return start, finish


def low_sum(ref, size):
    value = ref[0].astype(jnp.float32)
    for index in range(1, size):
        value = value + ref[index].astype(jnp.float32)
    return value


def kernel(
    plan,
    queries,
    keys,
    values,
    grads,
    key_weight,
    value_weight,
    key_up,
    value_up,
    out_weight,
    normed_whole,
    scale,
    gain,
    key_down,
    value_down,
    grad_query,
    grad_hidden,
    grad_text,
    key_down_grad,
    value_down_grad,
    key_up_grad,
    value_up_grad,
    part,
    up_in,
    up_out,
    down_in,
    down_out,
    total,
    project,
    context_all,
    project_all,
    text,
    sum_all,
    latent_own,
    latent_all,
    latent,
    up_sum,
    up_own,
    up_all,
    rows_all,
    up_whole,
    down_sum,
    down_all,
    up_send,
    up_recv,
    down_send,
    down_recv,
    context_send,
    context_recv,
    project_send,
    project_recv,
    sum_send,
    sum_recv,
    latent_send,
    latent_recv,
    up_dp_send,
    up_dp_recv,
    down_dp_send,
    down_dp_recv,
    rows_send,
    rows_recv,
    whole_send,
    whole_recv,
    near_up_send,
    near_up_recv,
    near_down_send,
    near_down_recv,
    text_sem,
    normed,
    normed_sem,
):
    n, splits, prompts = plan["n"], plan["splits"], plan["prompts"]
    heads, slices, lag = plan["heads"], plan["slices"], plan["lag"]
    first, second, steps = plan["first"], plan["second"], plan["steps"]
    length, features = normed.shape
    block = length // n
    sub = block // 2
    half_length = length // 2
    rank = key_down.shape[0]
    step = pl.program_id(0)
    me = lax.axis_index("seq")
    split = lax.axis_index("tp")
    prompt = lax.axis_index("dp")
    factor = HD ** (-0.5)
    above = lax.rem(me + 1, n)
    below = lax.rem(me + n - 1, n)
    has_low = me > 0
    has_high = me < n - 1

    def rows_of(value, half):
        return jnp.concatenate(
            [
                value[owner * block + half * sub : owner * block + half * sub + sub]
                for owner in range(n)
            ],
            axis=0,
        )

    def context_of(half):
        return (rows_of(normed, half).astype(jnp.float32) * gain[...]).astype(LOW)

    def column(row, size):
        return jnp.transpose(jnp.broadcast_to(row, (128, size)))[:, :1]

    ring = plan["ring"]

    def heads_ring(half, index):
        return lax.rem(index + half * heads, ring)

    def hidden_ring(half, index):
        return lax.rem(first + index + half * (second - first), ring)

    def up_copy(half, index, source):
        return pltpu.make_async_remote_copy(
            src_ref=source.at[half, index],
            dst_ref=up_in.at[half, index],
            send_sem=up_send.at[heads_ring(half, index)],
            recv_sem=up_recv.at[heads_ring(half, index)],
            device_id={"seq": above},
            device_id_type=MESH,
        )

    def down_copy(half, index, source):
        return pltpu.make_async_remote_copy(
            src_ref=source.at[half, index],
            dst_ref=down_in.at[half, index],
            send_sem=down_send.at[heads_ring(half, index)],
            recv_sem=down_recv.at[heads_ring(half, index)],
            device_id={"seq": below},
            device_id_type=MESH,
        )

    def high_copy(half, index, source, owner):
        rows = pl.ds(owner * sub, (n - owner) * sub)
        return pltpu.make_async_remote_copy(
            src_ref=source.at[half, index, :, rows],
            dst_ref=up_in.at[half, index, :, rows],
            send_sem=up_send.at[hidden_ring(half, index)],
            recv_sem=up_recv.at[hidden_ring(half, index)],
            device_id={"seq": above},
            device_id_type=MESH,
        )

    def low_copy(half, index, source, owner):
        rows = pl.ds(0, (owner + 1) * sub)
        return pltpu.make_async_remote_copy(
            src_ref=source.at[half, index, :, rows],
            dst_ref=down_in.at[half, index, :, rows],
            send_sem=down_send.at[hidden_ring(half, index)],
            recv_sem=down_recv.at[hidden_ring(half, index)],
            device_id={"seq": below},
            device_id_type=MESH,
        )

    def near_up_copy(half, index):
        rows = pl.ds(sub, sub)
        return pltpu.make_async_remote_copy(
            src_ref=part.at[half, index, :, rows],
            dst_ref=up_in.at[half, index, :, rows],
            send_sem=near_up_send.at[hidden_ring(half, index)],
            recv_sem=near_up_recv.at[hidden_ring(half, index)],
            device_id={"seq": above},
            device_id_type=MESH,
        )

    def near_down_copy(half, index):
        rows = pl.ds((n - 2) * sub, sub)
        return pltpu.make_async_remote_copy(
            src_ref=part.at[half, index, :, rows],
            dst_ref=down_in.at[half, index, :, rows],
            send_sem=near_down_send.at[hidden_ring(half, index)],
            recv_sem=near_down_recv.at[hidden_ring(half, index)],
            device_id={"seq": below},
            device_id_type=MESH,
        )

    def attend(position):
        live = jnp.logical_and(position >= 0, position < 2 * heads)
        half = (position >= heads).astype(jnp.int32)
        return live, half, position - half * heads

    def hide(position):
        live = jnp.logical_or(
            jnp.logical_and(position >= first, position < first + slices),
            jnp.logical_and(position >= second, position < second + slices),
        )
        half = (position >= second).astype(jnp.int32)
        return live, half, position - first - half * (second - first)

    @pl.when(step == 0)
    def _():
        barrier = pltpu.get_barrier_semaphore()
        for axis, size in (("seq", n), ("dp", prompts), ("tp", splits)):
            for offset in reversed(range(1, size)):
                pl.semaphore_signal(
                    barrier,
                    inc=1,
                    device_id={axis: lax.rem(lax.axis_index(axis) + offset, size)},
                    device_id_type=MESH,
                )
        pltpu.make_async_copy(normed_whole, normed, normed_sem).start()

    @pl.when(step < heads)
    def _():
        query, key, value, grad = queries[...], keys[...], values[...], grads[...]
        scores = dot(key, query, 1, 1) * factor
        weights = jnp.exp(scores - jnp.max(scores, axis=0, keepdims=True))
        probability = weights * (1.0 / jnp.sum(weights, axis=0, keepdims=True))
        value_part = dot(probability.astype(LOW), grad, 1, 0).astype(LOW)
        grad_probs = dot(value, grad, 1, 1)
        grad_scores = probability * (
            grad_probs - jnp.sum(probability * grad_probs, axis=0, keepdims=True)
        )
        grad_low = grad_scores.astype(LOW)
        key_part = (dot(grad_low, query, 1, 0) * factor).astype(LOW)
        for kind, side in ((0, key_part), (1, value_part)):
            for half in range(2):
                part[half, step, kind] = rows_of(side, half)
        grad_query[...] = (dot(grad_low, key, 0, 0) * factor).astype(LOW)

    @pl.when(step == 0)
    def _():
        pl.semaphore_wait(pltpu.get_barrier_semaphore(), splits + n + prompts - 3)

    live, half, index = hide(step)

    @pl.when(live)
    def _():
        product = dot(text[half].reshape(half_length, features), out_weight[...], 1, 1)
        product = product.astype(LOW)
        part[half, index, 0] = product[:, :HD]
        part[half, index, 1] = product[:, HD:]

    up_at = step - plan["spacing"] * me
    down_at = step - plan["spacing"] * (n - 1 - me)

    live, half, index = attend(up_at)

    @pl.when(jnp.logical_and(live, me == 0))
    def _():
        up_copy(half, index, part).start()
        up_in[half, index] = jnp.zeros(up_in.shape[2:], LOW)

    @pl.when(jnp.logical_and(live, has_low))
    def _():
        up_copy(half, index, up_out).wait_recv()

        @pl.when(has_high)
        def _():
            up_out[half, index] = up_in[half, index] + part[half, index]
            up_copy(half, index, up_out).start()

    live, half, index = attend(down_at)

    @pl.when(jnp.logical_and(live, me == n - 1))
    def _():
        down_copy(half, index, part).start()
        down_in[half, index] = jnp.zeros(down_in.shape[2:], LOW)

    @pl.when(jnp.logical_and(live, has_high))
    def _():
        down_copy(half, index, down_out).wait_recv()

        @pl.when(has_low)
        def _():
            down_out[half, index] = down_in[half, index] + part[half, index]
            down_copy(half, index, down_out).start()

    live, half, index = hide(up_at)
    for place in range(n):

        @pl.when(jnp.logical_and(live, me == place))
        def _():
            if place == 0:
                up_in[half, index, :, :sub] = jnp.zeros((2, sub, HD), LOW)
                if n > 2:
                    high_copy(half, index, part, 2).start()
            elif place == 1:
                if n > 2:
                    high_copy(half, index, up_out, 2).wait_recv()
            else:
                high_copy(half, index, up_out, place).wait_recv()
            if 0 < place < n - 1:
                rest = (place + 1) * sub
                up_out[half, index, :, rest:] = (
                    up_in[half, index, :, rest:] + part[half, index, :, rest:]
                )
                high_copy(half, index, up_out, place + 1).start()

    live, half, index = hide(down_at)
    for place in range(n):

        @pl.when(jnp.logical_and(live, me == place))
        def _():
            if place == n - 1:
                down_in[half, index, :, place * sub :] = jnp.zeros((2, sub, HD), LOW)
                if n > 2:
                    low_copy(half, index, part, n - 3).start()
            elif place == n - 2:
                if n > 2:
                    low_copy(half, index, down_out, n - 3).wait_recv()
            else:
                low_copy(half, index, down_out, place).wait_recv()
            if 0 < place < n - 1:
                rest = place * sub
                down_out[half, index, :, :rest] = (
                    down_in[half, index, :, :rest] + part[half, index, :, :rest]
                )
                low_copy(half, index, down_out, place - 1).start()

    live, half, index = hide(step - plan["delay"])

    @pl.when(jnp.logical_and(live, me == 0))
    def _():
        near_up_copy(half, index).start()

    @pl.when(jnp.logical_and(live, me == n - 1))
    def _():
        near_down_copy(half, index).start()

    @pl.when(step == 0)
    def _():
        total[...] = jnp.zeros_like(total)
        project[...] = jnp.zeros_like(project)
        up_sum[...] = jnp.zeros_like(up_sum)

    def latent_copy(slot, owner, offset):
        return pltpu.make_async_remote_copy(
            src_ref=latent_own.at[owner],
            dst_ref=latent_all.at[slot],
            send_sem=latent_send.at[offset],
            recv_sem=latent_recv.at[slot],
            device_id={"seq": lax.rem(me + offset, n)},
            device_id_type=MESH,
        )

    @pl.when(step == 1)
    def _():
        pltpu.make_async_copy(normed_whole, normed, normed_sem).wait()
        down = jnp.concatenate([key_down[...], value_down[...]], axis=0)
        sides = [dot(down, context_of(side), 1, 1) for side in range(2)]
        latent_own[...] = (
            jnp.concatenate(sides, axis=1).reshape(latent_own.shape).astype(LOW)
        )
        for offset in range(1, n):
            latent_copy(me, lax.rem(me + offset, n), offset).start()
        latent_all[me] = latent_own[me]

    @pl.when(step == lag - 1)
    def _():
        for offset in range(1, n):
            latent_copy(lax.rem(me + offset, n), me, offset).wait_recv()
        for offset in range(1, n):
            latent_copy(me, lax.rem(me + offset, n), offset).wait_send()
        both = low_sum(latent_all, n).astype(LOW)
        for side in range(2):
            latent[side] = both[:, side * half_length : (side + 1) * half_length]

    live, half, index = attend(step - lag)

    @pl.when(live)
    def _():
        @pl.when(has_high)
        def _():
            up_copy(half, index, up_out).wait_send()

        @pl.when(has_low)
        def _():
            down_copy(half, index, down_out).wait_send()

        both = (
            up_in[half, index].astype(jnp.float32)
            + part[half, index].astype(jnp.float32)
            + down_in[half, index].astype(jnp.float32)
        ).astype(LOW)
        pair = jnp.concatenate([both[0], both[1]], axis=1)
        slab = jnp.concatenate([key_weight[...], value_weight[...]], axis=1)
        total[half] += dot(pair, slab, 1, 1)
        blank = jnp.zeros((rank, HD), LOW)
        rises = jnp.concatenate(
            [
                jnp.concatenate([key_up[...], blank], axis=1),
                jnp.concatenate([blank, value_up[...]], axis=1),
            ],
            axis=0,
        )
        project[half] += dot(pair, rises, 1, 1)
        own = jnp.where(me < n // 2, both[0], both[1])
        up_sum[index] += dot(latent[half], own, 1, 0)

    for side in range(2):
        end = heads * (side + 1) + lag - 1
        project_start, project_finish = exchange(
            "tp", splits, project_all.at[side], project_send.at[side], project_recv.at[side]
        )
        context_start, context_finish = exchange(
            "tp", splits, context_all.at[side], context_send.at[side], context_recv.at[side]
        )
        sum_start, sum_finish = exchange(
            "seq", n, sum_all.at[side], sum_send.at[side], sum_recv.at[side]
        )

        @pl.when(step == end)
        def _():
            project_all[side, split] = project[side].astype(LOW)
            context_all[side, split] = total[side].astype(LOW)
            project_start()
            context_start()

        @pl.when(step == end + 2)
        def _():
            project_finish()
            context_finish()
            back = low_sum(project_all.at[side], splits).astype(LOW)
            low_rank = dot(back[:, :rank], key_down[...], 1, 0) + dot(
                back[:, rank:], value_down[...], 1, 0
            )
            scaled = gain[...] * (low_sum(context_all.at[side], splits) + low_rank)
            total[side] = scaled
            local_sum = jnp.sum(
                rows_of(normed, side).astype(jnp.float32) * scaled, axis=1, keepdims=True
            )
            line = jnp.transpose(jnp.broadcast_to(local_sum, (half_length, 128)))[:1, :]
            sum_all[side, me] = jnp.concatenate(
                [line[:, at : at + 128] for at in range(0, half_length, 128)], axis=0
            )
            sum_start()
            down = dot(back, context_of(side), 0, 0)
            if side == 0:
                down_sum[...] = down
            else:
                down_sum[...] += down

        @pl.when(step == end + 6)
        def _():
            sum_finish()
            token_sum = sum_all[side, 0]
            for other in range(1, n):
                token_sum = token_sum + sum_all[side, other]
            line = jnp.concatenate(
                [token_sum[at : at + 1] for at in range(half_length // 128)], axis=1
            )
            token_column = column(line, half_length)
            result = rows_of(column(scale[...], length), side) * (
                total[side]
                - rows_of(normed, side).astype(jnp.float32)
                * (token_column / plan["features_whole"])
            )
            text[side] = result.astype(LOW).reshape(n, sub, features)
            for owner in range(n):
                pltpu.make_async_copy(
                    text.at[side, owner],
                    grad_text.at[pl.ds(owner * block + side * sub, sub)],
                    text_sem.at[side, owner],
                ).start()

    end = 2 * heads + lag - 1
    portion = up_own.shape[2]

    def up_piece(slot, owner, offset):
        return pltpu.make_async_remote_copy(
            src_ref=up_own.at[owner],
            dst_ref=up_all.at[slot],
            send_sem=up_dp_send.at[offset],
            recv_sem=up_dp_recv.at[slot],
            device_id={"dp": lax.rem(prompt + offset, prompts)},
            device_id_type=MESH,
        )

    whole_start, whole_finish = exchange("dp", prompts, up_whole, whole_send, whole_recv)
    down_start, down_finish = exchange("dp", prompts, down_all, down_dp_send, down_dp_recv)
    rows_start, rows_finish = exchange("seq", n, rows_all, rows_send, rows_recv)

    @pl.when(step == end + 1)
    def _():
        rows = jnp.concatenate([up_sum[index] for index in range(heads)], axis=1).astype(LOW)
        for owner in range(prompts):
            up_own[owner] = rows[:, owner * portion : (owner + 1) * portion]
        for offset in range(1, prompts):
            up_piece(prompt, lax.rem(prompt + offset, prompts), offset).start()
        up_all[prompt] = up_own[prompt]

    @pl.when(step == end + 3)
    def _():
        down_all[prompt] = down_sum[...].astype(LOW)
        down_start()

    @pl.when(step == end + 5)
    def _():
        for offset in range(1, prompts):
            up_piece(lax.rem(prompt + offset, prompts), prompt, offset).wait_recv()
        for offset in range(1, prompts):
            up_piece(prompt, lax.rem(prompt + offset, prompts), offset).wait_send()
        rows_all[me] = (low_sum(up_all, prompts) / prompts).astype(LOW)
        rows_start()

    @pl.when(step == end + 9)
    def _():
        down_finish()
        down = low_sum(down_all, prompts)
        key_down_grad[...] = down[:rank] / prompts
        value_down_grad[...] = down[rank:] / prompts

    @pl.when(step == end + 12)
    def _():
        rows_finish()
        up_whole[prompt] = rows_all[...]
        whole_start()

    @pl.when(step == end + 18)
    def _():
        whole_finish()
        for owner in range(prompts):
            columns = slice(owner * portion, (owner + 1) * portion)
            rows = up_whole[owner].astype(jnp.float32).reshape(2 * rank, portion)
            key_up_grad[:, columns] = rows[:rank]
            value_up_grad[:, columns] = rows[rank:]

    live, half, index = hide(step - lag)
    for place in range(n):

        @pl.when(jnp.logical_and(live, me == place))
        def _():
            if place == 0:
                near_up_copy(half, index).wait_send()
            if place == 1:
                near_up_copy(half, index).wait_recv()
            if place == n - 2:
                near_down_copy(half, index).wait_recv()
            if place == n - 1:
                near_down_copy(half, index).wait_send()
            if place < n - 1 and n > 2:
                high_copy(half, index, up_out, max(place + 1, 2)).wait_send()
            if place > 0 and n > 2:
                low_copy(half, index, down_out, min(place - 1, n - 3)).wait_send()
            own = slice(place * sub, (place + 1) * sub)
            both = (
                up_in[half, index, :, own].astype(jnp.float32)
                + part[half, index, :, own].astype(jnp.float32)
                + down_in[half, index, :, own].astype(jnp.float32)
            ).astype(LOW)
            grad_hidden[...] = jnp.concatenate([both[0], both[1]], axis=1)

    @pl.when(step == steps - 1)
    def _():
        for side in range(2):
            for owner in range(n):
                pltpu.make_async_copy(
                    text.at[side, owner],
                    grad_text.at[pl.ds(owner * block + side * sub, sub)],
                    text_sem.at[side, owner],
                ).wait()


def store_kernel(count, pieces, *refs):
    sources, results, stages = refs[:count], refs[count : 2 * count], refs[2 * count : 3 * count]
    load_sem, store_sem = refs[3 * count :]

    def copies(item, piece):
        rows = sources[item].shape[0] // pieces[item]
        at = pl.ds(piece * rows, rows)
        slot = sum(pieces[:item]) + piece
        return (
            pltpu.make_async_copy(
                sources[item].at[at], stages[item].at[at], load_sem.at[slot]
            ),
            pltpu.make_async_copy(
                stages[item].at[at], results[item].at[at], store_sem.at[slot]
            ),
        )

    every = [copies(item, piece) for item in range(count) for piece in range(pieces[item])]
    for load, _ in every:
        load.start()
    for load, store in every:
        load.wait()
        store.start()
    for _, store in every:
        store.wait()


def store(*arrays):
    pieces = [1] * len(arrays)
    total = sum(pieces)
    anywhere = pl.BlockSpec(memory_space=pl.ANY)
    return pl.pallas_call(
        functools.partial(store_kernel, len(arrays), pieces),
        out_shape=tuple(jax.ShapeDtypeStruct(value.shape, value.dtype) for value in arrays),
        in_specs=[anywhere] * len(arrays),
        out_specs=(anywhere,) * len(arrays),
        scratch_shapes=[pltpu.VMEM(value.shape, value.dtype) for value in arrays]
        + [pltpu.SemaphoreType.DMA((total,))] * 2,
        name="store",
    )(*arrays)


def shards(
    queries,
    keys,
    values,
    grad_attention,
    normed,
    norm_scale,
    norm_gain,
    key_weight,
    value_weight,
    key_down,
    key_up,
    value_down,
    value_up,
    out_weight,
):
    rows, columns = queries.shape[1:]
    length, features = normed.shape[1:]
    rank = key_up.shape[0]
    hidden = out_weight.shape[0]
    n, splits, prompts = lax.axis_size("seq"), lax.axis_size("tp"), lax.axis_size("dp")
    heads = columns // HD
    width = 2 * HD
    slices = hidden // width
    spacing = 3
    lag = spacing * (n - 1)
    first = max(2 * heads, heads + lag + 6)
    second = max(first + slices, 2 * heads + lag + 6)
    steps = max(second + slices + lag, 2 * heads + lag + 18)
    ring = lag + spacing + 2
    block = length // n
    sub = block // 2
    half_length = length // 2
    share = 2 * rank // n
    plan = dict(
        n=n,
        splits=splits,
        prompts=prompts,
        heads=heads,
        slices=slices,
        lag=lag,
        spacing=spacing,
        ring=ring,
        delay=max(0, min(4, lag - 2)),
        first=first,
        second=second,
        steps=steps,
        features_whole=features * n,
    )

    def early(height):
        return pl.BlockSpec((height, HD), lambda step: (0, jnp.minimum(step, heads - 1)))

    def late(height):
        def place(step):
            at = jnp.clip(step - lag, 0, 2 * heads - 1)
            return 0, at - jnp.where(at >= heads, heads, 0)

        return pl.BlockSpec((height, HD), place)

    def fixed(height, size):
        return pl.BlockSpec((height, size), lambda step: (0, 0))

    def slice_of(step):
        after = step >= second
        return after.astype(jnp.int32), jnp.clip(
            step - jnp.where(after, second, first), 0, slices - 1
        )

    buffer = pltpu.VMEM((2, max(heads, slices), 2, half_length, HD), LOW)
    dma = pltpu.SemaphoreType.DMA
    grad_query, grad_hidden, grad_text, down_key, down_value, up_key, up_value = pl.pallas_call(
        functools.partial(kernel, plan),
        grid=(steps,),
        out_shape=(
            jax.ShapeDtypeStruct((rows, columns), LOW),
            jax.ShapeDtypeStruct((block, hidden), LOW),
            jax.ShapeDtypeStruct((length, features), LOW),
            jax.ShapeDtypeStruct((rank, features), jnp.float32),
            jax.ShapeDtypeStruct((rank, features), jnp.float32),
            jax.ShapeDtypeStruct((rank, columns), jnp.float32),
            jax.ShapeDtypeStruct((rank, columns), jnp.float32),
        ),
        in_specs=[
            early(rows),
            early(length),
            early(length),
            early(rows),
            late(features),
            late(features),
            late(rank),
            late(rank),
            pl.BlockSpec((width, features), lambda step: (slice_of(step)[1], 0)),
            pl.BlockSpec(memory_space=pl.ANY),
            fixed(1, length),
            fixed(1, features),
            fixed(rank, features),
            fixed(rank, features),
        ],
        out_specs=(
            early(rows),
            pl.BlockSpec((sub, width), lambda step: slice_of(step - lag)),
            pl.BlockSpec(memory_space=pl.ANY),
            fixed(rank, features),
            fixed(rank, features),
            fixed(rank, columns),
            fixed(rank, columns),
        ),
        scratch_shapes=[buffer] * 5
        + [
            pltpu.VMEM((2, half_length, features), jnp.float32),
            pltpu.VMEM((2, half_length, 2 * rank), jnp.float32),
            pltpu.VMEM((2, splits, half_length, features), LOW),
            pltpu.VMEM((2, splits, half_length, 2 * rank), LOW),
            pltpu.VMEM((2, n, sub, features), LOW),
            pltpu.VMEM((2, n, half_length // 128, 128), jnp.float32),
            pltpu.VMEM((n, share, length), LOW),
            pltpu.VMEM((n, share, length), LOW),
            pltpu.VMEM((2, share, half_length), LOW),
            pltpu.VMEM((heads, share, HD), jnp.float32),
            pltpu.VMEM((prompts, share, columns // prompts), LOW),
            pltpu.VMEM((prompts, share, columns // prompts), LOW),
            pltpu.VMEM((n, share, columns // prompts), LOW),
            pltpu.VMEM((prompts, n, share, columns // prompts), LOW),
            pltpu.VMEM((2 * rank, features), jnp.float32),
            pltpu.VMEM((prompts, 2 * rank, features), LOW),
        ]
        + [dma((ring,))] * 4
        + [dma((2, splits))] * 4
        + [dma((2, n))] * 2
        + [dma((n,))] * 2
        + [dma((prompts,))] * 4
        + [dma((n,))] * 2
        + [dma((prompts,))] * 2
        + [dma((ring,))] * 4
        + [dma((2, n))]
        + [pltpu.VMEM((length, features), LOW), dma],
        compiler_params=pltpu.CompilerParams(
            collective_id=0, has_side_effects=True, vmem_limit_bytes=62 * 1024 * 1024
        ),
        name="fused",
    )(
        queries[0],
        keys[0],
        values[0],
        grad_attention[0],
        key_weight,
        value_weight,
        key_up,
        value_up,
        out_weight,
        normed[0],
        norm_scale,
        norm_gain[None, :],
        key_down.T,
        value_down.T,
    )
    grad_query, grad_hidden, grad_text, down_key, down_value, up_key, up_value = store(
        grad_query, grad_hidden, grad_text, down_key, down_value, up_key, up_value
    )
    return (
        grad_query[None],
        grad_text[None],
        grad_hidden[None],
        down_key.T,
        up_key,
        down_value.T,
        up_value,
    )


def solution(mesh):
    return jax.shard_map(
        shards,
        mesh=mesh,
        in_specs=(
            P("dp", "seq", "tp"),
            P("dp", None, "tp"),
            P("dp", None, "tp"),
            P("dp", "seq", "tp"),
            P("dp", None, "seq"),
            P("dp", None),
            P("seq"),
            P("seq", "tp"),
            P("seq", "tp"),
            P("seq", None),
            P(None, "tp"),
            P("seq", None),
            P(None, "tp"),
            P("tp", "seq"),
        ),
        out_specs=(
            P("dp", "seq", "tp"),
            P("dp", None, "seq"),
            P("dp", "seq", "tp"),
            P("seq", None),
            P(None, "tp"),
            P("seq", None),
            P(None, "tp"),
        ),
        check_vma=False,
    )
```

```python
import functools

import jax
import jax.numpy as jnp
from jax import lax
from jax.experimental import pallas as pl
from jax.experimental.pallas import tpu as pltpu
from jax.sharding import PartitionSpec as P

HD = 128
MESH = pl.DeviceIdType.MESH
LOW = jnp.bfloat16


def dot(left_side, right_side, left_dim, right_dim):
    return lax.dot_general(
        left_side,
        right_side,
        (((left_dim,), (right_dim,)), ((), ())),
        preferred_element_type=jnp.float32,
    )


def exchange(axis, size, landing, send, recv):
    me = lax.axis_index(axis)

    def copy(slot, offset):
        return pltpu.make_async_remote_copy(
            src_ref=landing.at[slot],
            dst_ref=landing.at[slot],
            send_sem=send.at[offset],
            recv_sem=recv.at[slot],
            device_id={axis: lax.rem(me + offset, size)},
            device_id_type=MESH,
        )

    def start():
        for offset in range(1, size):
            copy(me, offset).start()

    def finish():
        for offset in range(1, size):
            copy(lax.rem(me + offset, size), offset).wait_recv()
        for offset in range(1, size):
            copy(me, offset).wait_send()

    return start, finish


def low_sum(ref, size):
    value = ref[0].astype(jnp.float32)
    for index in range(1, size):
        value = value + ref[index].astype(jnp.float32)
    return value


def kernel(
    plan,
    queries,
    keys,
    values,
    grads,
    key_weight,
    value_weight,
    key_up,
    value_up,
    out_weight,
    normed_whole,
    scale,
    gain,
    key_down,
    value_down,
    grad_query,
    grad_hidden,
    grad_text,
    key_down_grad,
    value_down_grad,
    key_up_grad,
    value_up_grad,
    part,
    up_in,
    up_out,
    down_in,
    down_out,
    total,
    project,
    context_all,
    project_all,
    text,
    sum_all,
    latent_own,
    latent_all,
    latent,
    up_sum,
    up_own,
    up_all,
    rows_all,
    up_whole,
    down_sum,
    down_all,
    up_send,
    up_recv,
    down_send,
    down_recv,
    context_send,
    context_recv,
    project_send,
    project_recv,
    sum_send,
    sum_recv,
    latent_send,
    latent_recv,
    up_dp_send,
    up_dp_recv,
    down_dp_send,
    down_dp_recv,
    rows_send,
    rows_recv,
    whole_send,
    whole_recv,
    near_up_send,
    near_up_recv,
    near_down_send,
    near_down_recv,
    text_sem,
    normed,
    normed_sem,
):
    n, splits, prompts = plan["n"], plan["splits"], plan["prompts"]
    heads, slices, lag = plan["heads"], plan["slices"], plan["lag"]
    first, second, steps = plan["first"], plan["second"], plan["steps"]
    length, features = normed.shape
    block = length // n
    sub = block // 2
    half_length = length // 2
    rank = key_down.shape[0]
    step = pl.program_id(0)
    me = lax.axis_index("seq")
    split = lax.axis_index("tp")
    prompt = lax.axis_index("dp")
    factor = HD ** (-0.5)
    above = lax.rem(me + 1, n)
    below = lax.rem(me + n - 1, n)
    has_low = me > 0
    has_high = me < n - 1

    def rows_of(value, half):
        return jnp.concatenate(
            [
                value[owner * block + half * sub : owner * block + half * sub + sub]
                for owner in range(n)
            ],
            axis=0,
        )

    def context_of(half):
        return (rows_of(normed, half).astype(jnp.float32) * gain[...]).astype(LOW)

    def column(row, size):
        return jnp.transpose(jnp.broadcast_to(row, (128, size)))[:, :1]

    ring = plan["ring"]

    def heads_ring(half, index):
        return lax.rem(index + half * heads, ring)

    def hidden_ring(half, index):
        return lax.rem(first + index + half * (second - first), ring)

    def up_copy(half, index, source):
        return pltpu.make_async_remote_copy(
            src_ref=source.at[half, index],
            dst_ref=up_in.at[half, index],
            send_sem=up_send.at[heads_ring(half, index)],
            recv_sem=up_recv.at[heads_ring(half, index)],
            device_id={"seq": above},
            device_id_type=MESH,
        )

    def down_copy(half, index, source):
        return pltpu.make_async_remote_copy(
            src_ref=source.at[half, index],
            dst_ref=down_in.at[half, index],
            send_sem=down_send.at[heads_ring(half, index)],
            recv_sem=down_recv.at[heads_ring(half, index)],
            device_id={"seq": below},
            device_id_type=MESH,
        )

    def high_copy(half, index, source, owner):
        rows = pl.ds(owner * sub, (n - owner) * sub)
        return pltpu.make_async_remote_copy(
            src_ref=source.at[half, index, :, rows],
            dst_ref=up_in.at[half, index, :, rows],
            send_sem=up_send.at[hidden_ring(half, index)],
            recv_sem=up_recv.at[hidden_ring(half, index)],
            device_id={"seq": above},
            device_id_type=MESH,
        )

    def low_copy(half, index, source, owner):
        rows = pl.ds(0, (owner + 1) * sub)
        return pltpu.make_async_remote_copy(
            src_ref=source.at[half, index, :, rows],
            dst_ref=down_in.at[half, index, :, rows],
            send_sem=down_send.at[hidden_ring(half, index)],
            recv_sem=down_recv.at[hidden_ring(half, index)],
            device_id={"seq": below},
            device_id_type=MESH,
        )

    def near_up_copy(half, index):
        rows = pl.ds(sub, sub)
        return pltpu.make_async_remote_copy(
            src_ref=part.at[half, index, :, rows],
            dst_ref=up_in.at[half, index, :, rows],
            send_sem=near_up_send.at[hidden_ring(half, index)],
            recv_sem=near_up_recv.at[hidden_ring(half, index)],
            device_id={"seq": above},
            device_id_type=MESH,
        )

    def near_down_copy(half, index):
        rows = pl.ds((n - 2) * sub, sub)
        return pltpu.make_async_remote_copy(
            src_ref=part.at[half, index, :, rows],
            dst_ref=down_in.at[half, index, :, rows],
            send_sem=near_down_send.at[hidden_ring(half, index)],
            recv_sem=near_down_recv.at[hidden_ring(half, index)],
            device_id={"seq": below},
            device_id_type=MESH,
        )

    def attend(position):
        live = jnp.logical_and(position >= 0, position < 2 * heads)
        half = (position >= heads).astype(jnp.int32)
        return live, half, position - half * heads

    def hide(position):
        live = jnp.logical_or(
            jnp.logical_and(position >= first, position < first + slices),
            jnp.logical_and(position >= second, position < second + slices),
        )
        half = (position >= second).astype(jnp.int32)
        return live, half, position - first - half * (second - first)

    @pl.when(step == 0)
    def _():
        barrier = pltpu.get_barrier_semaphore()
        for axis, size in (("seq", n), ("dp", prompts), ("tp", splits)):
            for offset in reversed(range(1, size)):
                pl.semaphore_signal(
                    barrier,
                    inc=1,
                    device_id={axis: lax.rem(lax.axis_index(axis) + offset, size)},
                    device_id_type=MESH,
                )
        pltpu.make_async_copy(normed_whole, normed, normed_sem).start()

    @pl.when(step < heads)
    def _():
        query, key, value, grad = queries[...], keys[...], values[...], grads[...]
        scores = dot(key, query, 1, 1)
        weights = jnp.exp((scores - jnp.max(scores, axis=0, keepdims=True)) * factor)
        probability = weights * (1.0 / jnp.sum(weights, axis=0, keepdims=True))
        value_part = dot(probability.astype(LOW), grad, 1, 0).astype(LOW)
        grad_probs = dot(value, grad, 1, 1)
        grad_scores = probability * (
            grad_probs - jnp.sum(probability * grad_probs, axis=0, keepdims=True)
        )
        grad_low = grad_scores.astype(LOW)
        key_part = (dot(grad_low, query, 1, 0) * factor).astype(LOW)
        for kind, side in ((0, key_part), (1, value_part)):
            for half in range(2):
                part[half, step, kind] = rows_of(side, half)
        grad_query[...] = (dot(grad_low, key, 0, 0) * factor).astype(LOW)

    @pl.when(step == 0)
    def _():
        pl.semaphore_wait(pltpu.get_barrier_semaphore(), splits + n + prompts - 3)

    live, half, index = hide(step)

    @pl.when(live)
    def _():
        product = dot(text[half].reshape(half_length, features), out_weight[...], 1, 1)
        product = product.astype(LOW)
        part[half, index, 0] = product[:, :HD]
        part[half, index, 1] = product[:, HD:]

    up_at = step - plan["spacing"] * me
    down_at = step - plan["spacing"] * (n - 1 - me)

    live, half, index = attend(up_at)

    @pl.when(jnp.logical_and(live, me == 0))
    def _():
        up_copy(half, index, part).start()
        up_in[half, index] = jnp.zeros(up_in.shape[2:], LOW)

    @pl.when(jnp.logical_and(live, has_low))
    def _():
        up_copy(half, index, up_out).wait_recv()

        @pl.when(has_high)
        def _():
            up_out[half, index] = up_in[half, index] + part[half, index]
            up_copy(half, index, up_out).start()

    live, half, index = attend(down_at)

    @pl.when(jnp.logical_and(live, me == n - 1))
    def _():
        down_copy(half, index, part).start()
        down_in[half, index] = jnp.zeros(down_in.shape[2:], LOW)

    @pl.when(jnp.logical_and(live, has_high))
    def _():
        down_copy(half, index, down_out).wait_recv()

        @pl.when(has_low)
        def _():
            down_out[half, index] = down_in[half, index] + part[half, index]
            down_copy(half, index, down_out).start()

    live, half, index = hide(up_at)
    for place in range(n):

        @pl.when(jnp.logical_and(live, me == place))
        def _():
            if place == 0:
                up_in[half, index, :, :sub] = jnp.zeros((2, sub, HD), LOW)
                if n > 2:
                    high_copy(half, index, part, 2).start()
            elif place == 1:
                if n > 2:
                    high_copy(half, index, up_out, 2).wait_recv()
            else:
                high_copy(half, index, up_out, place).wait_recv()
            if 0 < place < n - 1:
                rest = (place + 1) * sub
                up_out[half, index, :, rest:] = (
                    up_in[half, index, :, rest:] + part[half, index, :, rest:]
                )
                high_copy(half, index, up_out, place + 1).start()

    live, half, index = hide(down_at)
    for place in range(n):

        @pl.when(jnp.logical_and(live, me == place))
        def _():
            if place == n - 1:
                down_in[half, index, :, place * sub :] = jnp.zeros((2, sub, HD), LOW)
                if n > 2:
                    low_copy(half, index, part, n - 3).start()
            elif place == n - 2:
                if n > 2:
                    low_copy(half, index, down_out, n - 3).wait_recv()
            else:
                low_copy(half, index, down_out, place).wait_recv()
            if 0 < place < n - 1:
                rest = place * sub
                down_out[half, index, :, :rest] = (
                    down_in[half, index, :, :rest] + part[half, index, :, :rest]
                )
                low_copy(half, index, down_out, place - 1).start()

    live, half, index = hide(step - plan["delay"])

    @pl.when(jnp.logical_and(live, me == 0))
    def _():
        near_up_copy(half, index).start()

    @pl.when(jnp.logical_and(live, me == n - 1))
    def _():
        near_down_copy(half, index).start()

    @pl.when(step == 0)
    def _():
        total[...] = jnp.zeros_like(total)
        project[...] = jnp.zeros_like(project)
        up_sum[...] = jnp.zeros_like(up_sum)

    def latent_copy(slot, owner, offset):
        return pltpu.make_async_remote_copy(
            src_ref=latent_own.at[owner],
            dst_ref=latent_all.at[slot],
            send_sem=latent_send.at[offset],
            recv_sem=latent_recv.at[slot],
            device_id={"seq": lax.rem(me + offset, n)},
            device_id_type=MESH,
        )

    @pl.when(step == 1)
    def _():
        pltpu.make_async_copy(normed_whole, normed, normed_sem).wait()
        down = jnp.concatenate([key_down[...], value_down[...]], axis=0)
        sides = [dot(down, context_of(side), 1, 1) for side in range(2)]
        latent_own[...] = (
            jnp.concatenate(sides, axis=1).reshape(latent_own.shape).astype(LOW)
        )
        for offset in range(1, n):
            latent_copy(me, lax.rem(me + offset, n), offset).start()
        latent_all[me] = latent_own[me]

    @pl.when(step == lag - 1)
    def _():
        for offset in range(1, n):
            latent_copy(lax.rem(me + offset, n), me, offset).wait_recv()
        for offset in range(1, n):
            latent_copy(me, lax.rem(me + offset, n), offset).wait_send()
        both = low_sum(latent_all, n).astype(LOW)
        for side in range(2):
            latent[side] = both[:, side * half_length : (side + 1) * half_length]

    live, half, index = attend(step - lag)

    @pl.when(live)
    def _():
        @pl.when(has_high)
        def _():
            up_copy(half, index, up_out).wait_send()

        @pl.when(has_low)
        def _():
            down_copy(half, index, down_out).wait_send()

        both = (
            up_in[half, index].astype(jnp.float32)
            + part[half, index].astype(jnp.float32)
            + down_in[half, index].astype(jnp.float32)
        ).astype(LOW)
        pair = jnp.concatenate([both[0], both[1]], axis=1)
        slab = jnp.concatenate([key_weight[...], value_weight[...]], axis=1)
        total[half] += dot(pair, slab, 1, 1)
        blank = jnp.zeros((rank, HD), LOW)
        rises = jnp.concatenate(
            [
                jnp.concatenate([key_up[...], blank], axis=1),
                jnp.concatenate([blank, value_up[...]], axis=1),
            ],
            axis=0,
        )
        project[half] += dot(pair, rises, 1, 1)
        own = jnp.where(me < n // 2, both[0], both[1])
        up_sum[index] += dot(latent[half], own, 1, 0)

    for side in range(2):
        end = heads * (side + 1) + lag - 1
        project_start, project_finish = exchange(
            "tp", splits, project_all.at[side], project_send.at[side], project_recv.at[side]
        )
        context_start, context_finish = exchange(
            "tp", splits, context_all.at[side], context_send.at[side], context_recv.at[side]
        )
        sum_start, sum_finish = exchange(
            "seq", n, sum_all.at[side], sum_send.at[side], sum_recv.at[side]
        )

        @pl.when(step == end)
        def _():
            project_all[side, split] = project[side].astype(LOW)
            context_all[side, split] = total[side].astype(LOW)
            project_start()
            context_start()

        @pl.when(step == end + 2)
        def _():
            project_finish()
            context_finish()
            back = low_sum(project_all.at[side], splits).astype(LOW)
            low_rank = dot(back[:, :rank], key_down[...], 1, 0) + dot(
                back[:, rank:], value_down[...], 1, 0
            )
            scaled = gain[...] * (low_sum(context_all.at[side], splits) + low_rank)
            total[side] = scaled
            local_sum = jnp.sum(
                rows_of(normed, side).astype(jnp.float32) * scaled, axis=1, keepdims=True
            )
            line = jnp.transpose(jnp.broadcast_to(local_sum, (half_length, 128)))[:1, :]
            sum_all[side, me] = jnp.concatenate(
                [line[:, at : at + 128] for at in range(0, half_length, 128)], axis=0
            )
            sum_start()
            down = dot(back, context_of(side), 0, 0)
            if side == 0:
                down_sum[...] = down
            else:
                down_sum[...] += down

        @pl.when(step == end + 6)
        def _():
            sum_finish()
            token_sum = sum_all[side, 0]
            for other in range(1, n):
                token_sum = token_sum + sum_all[side, other]
            line = jnp.concatenate(
                [token_sum[at : at + 1] for at in range(half_length // 128)], axis=1
            )
            token_column = column(line, half_length)
            result = rows_of(column(scale[...], length), side) * (
                total[side]
                - rows_of(normed, side).astype(jnp.float32)
                * (token_column / plan["features_whole"])
            )
            text[side] = result.astype(LOW).reshape(n, sub, features)
            for owner in range(n):
                pltpu.make_async_copy(
                    text.at[side, owner],
                    grad_text.at[pl.ds(owner * block + side * sub, sub)],
                    text_sem.at[side, owner],
                ).start()

    end = 2 * heads + lag - 1
    portion = up_own.shape[2]

    def up_piece(slot, owner, offset):
        return pltpu.make_async_remote_copy(
            src_ref=up_own.at[owner],
            dst_ref=up_all.at[slot],
            send_sem=up_dp_send.at[offset],
            recv_sem=up_dp_recv.at[slot],
            device_id={"dp": lax.rem(prompt + offset, prompts)},
            device_id_type=MESH,
        )

    whole_start, whole_finish = exchange("dp", prompts, up_whole, whole_send, whole_recv)
    down_start, down_finish = exchange("dp", prompts, down_all, down_dp_send, down_dp_recv)
    rows_start, rows_finish = exchange("seq", n, rows_all, rows_send, rows_recv)

    @pl.when(step == end + 1)
    def _():
        rows = jnp.concatenate([up_sum[index] for index in range(heads)], axis=1).astype(LOW)
        for owner in range(prompts):
            up_own[owner] = rows[:, owner * portion : (owner + 1) * portion]
        for offset in range(1, prompts):
            up_piece(prompt, lax.rem(prompt + offset, prompts), offset).start()
        up_all[prompt] = up_own[prompt]

    @pl.when(step == end + 3)
    def _():
        down_all[prompt] = down_sum[...].astype(LOW)
        down_start()

    @pl.when(step == end + 5)
    def _():
        for offset in range(1, prompts):
            up_piece(lax.rem(prompt + offset, prompts), prompt, offset).wait_recv()
        for offset in range(1, prompts):
            up_piece(prompt, lax.rem(prompt + offset, prompts), offset).wait_send()
        rows_all[me] = (low_sum(up_all, prompts) / prompts).astype(LOW)
        rows_start()

    @pl.when(step == end + 9)
    def _():
        down_finish()
        down = low_sum(down_all, prompts)
        key_down_grad[...] = down[:rank] / prompts
        value_down_grad[...] = down[rank:] / prompts

    @pl.when(step == end + 12)
    def _():
        rows_finish()
        up_whole[prompt] = rows_all[...]
        whole_start()

    @pl.when(step == end + 18)
    def _():
        whole_finish()
        for owner in range(prompts):
            columns = slice(owner * portion, (owner + 1) * portion)
            rows = up_whole[owner].astype(jnp.float32).reshape(2 * rank, portion)
            key_up_grad[:, columns] = rows[:rank]
            value_up_grad[:, columns] = rows[rank:]

    live, half, index = hide(step - lag)
    for place in range(n):

        @pl.when(jnp.logical_and(live, me == place))
        def _():
            if place == 0:
                near_up_copy(half, index).wait_send()
            if place == 1:
                near_up_copy(half, index).wait_recv()
            if place == n - 2:
                near_down_copy(half, index).wait_recv()
            if place == n - 1:
                near_down_copy(half, index).wait_send()
            if place < n - 1 and n > 2:
                high_copy(half, index, up_out, max(place + 1, 2)).wait_send()
            if place > 0 and n > 2:
                low_copy(half, index, down_out, min(place - 1, n - 3)).wait_send()
            own = slice(place * sub, (place + 1) * sub)
            both = (
                up_in[half, index, :, own].astype(jnp.float32)
                + part[half, index, :, own].astype(jnp.float32)
                + down_in[half, index, :, own].astype(jnp.float32)
            ).astype(LOW)
            grad_hidden[...] = jnp.concatenate([both[0], both[1]], axis=1)

    @pl.when(step == steps - 1)
    def _():
        for side in range(2):
            for owner in range(n):
                pltpu.make_async_copy(
                    text.at[side, owner],
                    grad_text.at[pl.ds(owner * block + side * sub, sub)],
                    text_sem.at[side, owner],
                ).wait()


def store_kernel(count, pieces, *refs):
    sources, results, stages = refs[:count], refs[count : 2 * count], refs[2 * count : 3 * count]
    load_sem, store_sem = refs[3 * count :]

    def copies(item, piece):
        rows = sources[item].shape[0] // pieces[item]
        at = pl.ds(piece * rows, rows)
        slot = sum(pieces[:item]) + piece
        return (
            pltpu.make_async_copy(
                sources[item].at[at], stages[item].at[at], load_sem.at[slot]
            ),
            pltpu.make_async_copy(
                stages[item].at[at], results[item].at[at], store_sem.at[slot]
            ),
        )

    every = [copies(item, piece) for item in range(count) for piece in range(pieces[item])]
    for load, _ in every:
        load.start()
    for load, store in every:
        load.wait()
        store.start()
    for _, store in every:
        store.wait()


def store(*arrays):
    pieces = [1] * len(arrays)
    total = sum(pieces)
    anywhere = pl.BlockSpec(memory_space=pl.ANY)
    return pl.pallas_call(
        functools.partial(store_kernel, len(arrays), pieces),
        out_shape=tuple(jax.ShapeDtypeStruct(value.shape, value.dtype) for value in arrays),
        in_specs=[anywhere] * len(arrays),
        out_specs=(anywhere,) * len(arrays),
        scratch_shapes=[pltpu.VMEM(value.shape, value.dtype) for value in arrays]
        + [pltpu.SemaphoreType.DMA((total,))] * 2,
        name="store",
    )(*arrays)


def shards(
    queries,
    keys,
    values,
    grad_attention,
    normed,
    norm_scale,
    norm_gain,
    key_weight,
    value_weight,
    key_down,
    key_up,
    value_down,
    value_up,
    out_weight,
):
    rows, columns = queries.shape[1:]
    length, features = normed.shape[1:]
    rank = key_up.shape[0]
    hidden = out_weight.shape[0]
    n, splits, prompts = lax.axis_size("seq"), lax.axis_size("tp"), lax.axis_size("dp")
    heads = columns // HD
    width = 2 * HD
    slices = hidden // width
    spacing = 3
    lag = spacing * (n - 1)
    first = max(2 * heads, heads + lag + 6)
    second = max(first + slices, 2 * heads + lag + 6)
    steps = max(second + slices + lag, 2 * heads + lag + 18)
    ring = lag + spacing + 2
    block = length // n
    sub = block // 2
    half_length = length // 2
    share = 2 * rank // n
    plan = dict(
        n=n,
        splits=splits,
        prompts=prompts,
        heads=heads,
        slices=slices,
        lag=lag,
        spacing=spacing,
        ring=ring,
        delay=max(0, min(4, lag - 2)),
        first=first,
        second=second,
        steps=steps,
        features_whole=features * n,
    )

    def early(height):
        return pl.BlockSpec((height, HD), lambda step: (0, jnp.minimum(step, heads - 1)))

    def late(height):
        def place(step):
            at = jnp.clip(step - lag, 0, 2 * heads - 1)
            return 0, at - jnp.where(at >= heads, heads, 0)

        return pl.BlockSpec((height, HD), place)

    def fixed(height, size):
        return pl.BlockSpec((height, size), lambda step: (0, 0))

    def slice_of(step):
        after = step >= second
        return after.astype(jnp.int32), jnp.clip(
            step - jnp.where(after, second, first), 0, slices - 1
        )

    buffer = pltpu.VMEM((2, max(heads, slices), 2, half_length, HD), LOW)
    dma = pltpu.SemaphoreType.DMA
    grad_query, grad_hidden, grad_text, down_key, down_value, up_key, up_value = pl.pallas_call(
        functools.partial(kernel, plan),
        grid=(steps,),
        out_shape=(
            jax.ShapeDtypeStruct((rows, columns), LOW),
            jax.ShapeDtypeStruct((block, hidden), LOW),
            jax.ShapeDtypeStruct((length, features), LOW),
            jax.ShapeDtypeStruct((rank, features), jnp.float32),
            jax.ShapeDtypeStruct((rank, features), jnp.float32),
            jax.ShapeDtypeStruct((rank, columns), jnp.float32),
            jax.ShapeDtypeStruct((rank, columns), jnp.float32),
        ),
        in_specs=[
            early(rows),
            early(length),
            early(length),
            early(rows),
            late(features),
            late(features),
            late(rank),
            late(rank),
            pl.BlockSpec((width, features), lambda step: (slice_of(step)[1], 0)),
            pl.BlockSpec(memory_space=pl.ANY),
            fixed(1, length),
            fixed(1, features),
            fixed(rank, features),
            fixed(rank, features),
        ],
        out_specs=(
            early(rows),
            pl.BlockSpec((sub, width), lambda step: slice_of(step - lag)),
            pl.BlockSpec(memory_space=pl.ANY),
            fixed(rank, features),
            fixed(rank, features),
            fixed(rank, columns),
            fixed(rank, columns),
        ),
        scratch_shapes=[buffer] * 5
        + [
            pltpu.VMEM((2, half_length, features), jnp.float32),
            pltpu.VMEM((2, half_length, 2 * rank), jnp.float32),
            pltpu.VMEM((2, splits, half_length, features), LOW),
            pltpu.VMEM((2, splits, half_length, 2 * rank), LOW),
            pltpu.VMEM((2, n, sub, features), LOW),
            pltpu.VMEM((2, n, half_length // 128, 128), jnp.float32),
            pltpu.VMEM((n, share, length), LOW),
            pltpu.VMEM((n, share, length), LOW),
            pltpu.VMEM((2, share, half_length), LOW),
            pltpu.VMEM((heads, share, HD), jnp.float32),
            pltpu.VMEM((prompts, share, columns // prompts), LOW),
            pltpu.VMEM((prompts, share, columns // prompts), LOW),
            pltpu.VMEM((n, share, columns // prompts), LOW),
            pltpu.VMEM((prompts, n, share, columns // prompts), LOW),
            pltpu.VMEM((2 * rank, features), jnp.float32),
            pltpu.VMEM((prompts, 2 * rank, features), LOW),
        ]
        + [dma((ring,))] * 4
        + [dma((2, splits))] * 4
        + [dma((2, n))] * 2
        + [dma((n,))] * 2
        + [dma((prompts,))] * 4
        + [dma((n,))] * 2
        + [dma((prompts,))] * 2
        + [dma((ring,))] * 4
        + [dma((2, n))]
        + [pltpu.VMEM((length, features), LOW), dma],
        compiler_params=pltpu.CompilerParams(
            collective_id=0, has_side_effects=True, vmem_limit_bytes=62 * 1024 * 1024
        ),
        name="fused",
    )(
        queries[0],
        keys[0],
        values[0],
        grad_attention[0],
        key_weight,
        value_weight,
        key_up,
        value_up,
        out_weight,
        normed[0],
        norm_scale,
        norm_gain[None, :],
        key_down.T,
        value_down.T,
    )
    grad_query, grad_hidden, grad_text, down_key, down_value, up_key, up_value = store(
        grad_query, grad_hidden, grad_text, down_key, down_value, up_key, up_value
    )
    return (
        grad_query[None],
        grad_text[None],
        grad_hidden[None],
        down_key.T,
        up_key,
        down_value.T,
        up_value,
    )


def solution(mesh):
    return jax.shard_map(
        shards,
        mesh=mesh,
        in_specs=(
            P("dp", "seq", "tp"),
            P("dp", None, "tp"),
            P("dp", None, "tp"),
            P("dp", "seq", "tp"),
            P("dp", None, "seq"),
            P("dp", None),
            P("seq"),
            P("seq", "tp"),
            P("seq", "tp"),
            P("seq", None),
            P(None, "tp"),
            P("seq", None),
            P(None, "tp"),
            P("tp", "seq"),
        ),
        out_specs=(
            P("dp", "seq", "tp"),
            P("dp", None, "seq"),
            P("dp", "seq", "tp"),
            P("seq", None),
            P(None, "tp"),
            P("seq", None),
            P(None, "tp"),
        ),
        check_vma=False,
    )
```
